128 devices in a mesh: row: 16 (over x, y_lo, core), col: 8 (over y_hi, z).
Axes of the slice: x: 4, y: 4 (y_hi: 2, y_lo: 2; y = y_hi * 2 + y_lo), z: 4, core: 2. Of those that a mesh axis runs over, the one named last changes fastest.
Arguments:
- coarse_feats: bfloat16 [64, 1024], P(None, ('row', 'col')), may hold values from -6 to 6
- fine_feats: bfloat16 [64, 1024], P(None, ('row', 'col')), may hold values from -6 to 6
- pair_prior: bfloat16 [64, 1024, 1024], P(None, 'row', 'col'), may hold values from -6 to 6
- zoom_start: int32 [2], replicated, may hold values from 0 to 512, as said below
- coarse_weights: bfloat16 [2, 3, 64, 192], replicated, may hold values from -0.25 to 0.25
- coarse_bias: float32 [2, 64], replicated, may hold values from -2.5 to 2.5
- refine_first: bfloat16 [3, 64, 384], replicated, may hold values from -0.1875 to 0.1875
- refine_second: bfloat16 [3, 64, 192], replicated, may hold values from -0.25 to 0.25
- refine_bias: float32 [2, 64], replicated, may hold values from -2.5 to 2.5
Outputs:
- coarse_map: bfloat16 [64, 1024, 1024], P(None, 'row', 'col')
- refined: bfloat16 [64, 1024, 1024], P(None, 'row', 'col')
The draws below stay inside these ranges and needn't reach their ends.
Inputs may be any that keep to these rules, and one draw needn't show every extreme that they name: `zoom_start`: the two entries are 0 and 512 in either order.
All inputs are finite; a program needn't handle non-finite values.
Results may differ from the reference program's by a relative error of at most 0.0059.
Values may be sent and summed in bfloat16 or wider, within the bound.
A program may use at most 64 MiB of HBM per device.

```python
import jax
import jax.numpy as jnp
from jax import lax

C = 64
BINS = 1024


def draw_zoom_start(key, part):
    picked = jax.random.randint(key, (1,), 0, 2)
    both = jnp.concatenate([picked, 1 - picked])
    return (both * (BINS // 2)).astype(jnp.int32)


def block_levels(stream_key, extent, shards, low, largest):
    loudness, own = 1.0, jax.random.fold_in(stream_key, 6)
    for position, parts in shards:
        draws = jnp.exp(jax.random.uniform(jax.random.fold_in(own, position), (parts,), jnp.float32, low / len(shards), largest / len(shards)))
        loudness = loudness * jnp.repeat(draws, extent[position] // parts).reshape([-1 if axis == position else 1 for axis in range(len(extent))])
    return loudness


def centred(own_key, shape, deviation, most, split=(), kind=jnp.bfloat16):
    values = jax.random.normal(own_key, shape, jnp.float32) * deviation
    if len(split) > 0:
        values = block_levels(own_key, shape, split, -0.22, 0.18) * values
    return jnp.clip(values, min=-most, max=most).astype(kind)


def setup_inputs(seed: int = 0) -> dict:
    arg_keys = jax.random.split(jax.random.key(seed), 10)
    return {
        "coarse_feats": centred(arg_keys[0], (C, BINS), 1.0, 6.0, ((1, 128),)),
        "fine_feats": centred(arg_keys[1], (C, BINS), 1.0, 6.0, ((1, 128),)),
        "pair_prior": centred(arg_keys[2], (C, BINS, BINS), 1.0, 6.0, ((1, 16), (2, 8))),
        "zoom_start": draw_zoom_start(jax.random.fold_in(arg_keys[9], 71), 0),
        "coarse_weights": centred(arg_keys[4], (2, 3, C, 3 * C), (9 * C) ** -0.5, 0.25),
        "coarse_bias": centred(arg_keys[5], (2, C), 0.5, 2.5, (), jnp.float32),
        "refine_first": centred(arg_keys[6], (3, C, 6 * C), (18 * C) ** -0.5, 0.1875),
        "refine_second": centred(arg_keys[7], (3, C, 3 * C), (9 * C) ** -0.5, 0.25),
        "refine_bias": centred(arg_keys[8], (2, C), 0.5, 2.5, (), jnp.float32),
    }


def conv_layer(source, weights, biases, spacing):
    inputs = source.shape[0]
    outputs = weights.shape[1]
    kernel = weights.astype(jnp.float32).reshape(3, outputs, 3, inputs).transpose(1, 3, 0, 2)
    result = lax.conv_general_dilated(
        source.astype(jnp.float32)[None], kernel, (1, 1),
        [(spacing, spacing), (spacing, spacing)], rhs_dilation=(spacing, spacing),
        dimension_numbers=("NCHW", "OIHW", "NCHW"))[0]
    return jnp.maximum(result + biases.astype(jnp.float32)[:, None, None], 0.0).astype(jnp.bfloat16)


def reference(coarse_feats, fine_feats, pair_prior, zoom_start, coarse_weights, coarse_bias, refine_first, refine_second, refine_bias):
    coarse_wide = coarse_feats.astype(jnp.float32)
    pair_map = (coarse_wide[:, :, None] + coarse_wide[:, None, :] + pair_prior.astype(jnp.float32)).astype(jnp.bfloat16)
    hidden_coarse = conv_layer(pair_map, coarse_weights[0], coarse_bias[0], 2)
    coarse_map = conv_layer(hidden_coarse, coarse_weights[1], coarse_bias[1], 4)
    zoom_bin = zoom_start[0].astype(jnp.int32)
    window = lax.dynamic_slice(coarse_map, (jnp.int32(0), zoom_bin, zoom_bin), (C, BINS // 2, BINS // 2))
    window = jnp.repeat(jnp.repeat(window, 2, axis=1), 2, axis=2)
    fine_wide = fine_feats.astype(jnp.float32)
    fine_pair = (fine_wide[:, :, None] + fine_wide[:, None, :]).astype(jnp.bfloat16)
    joined = jnp.concatenate([window, fine_pair], axis=0)
    hidden_refine = conv_layer(joined, refine_first, refine_bias[0], 8)
    refined = conv_layer(hidden_refine, refine_second, refine_bias[1], 16)
    return coarse_map, refined
```

```python
import functools

import jax
import jax.numpy as jnp
import numpy as np
from jax import lax
from jax.experimental import pallas as pl
from jax.experimental.pallas import tpu as pltpu
from jax.sharding import PartitionSpec as P

BF = jnp.bfloat16
F32 = jnp.float32
MESH = pl.DeviceIdType.MESH
VMEM_BYTES = 58 << 20
SIDE = 1024
ROWS, COLS = 16, 8
TR, TC = 64, 128

vmem = pl.BlockSpec(memory_space=pltpu.VMEM)
anywhere = pl.BlockSpec(memory_space=pl.ANY)


def lanes_of(shape):
    return lax.broadcasted_iota(jnp.int32, shape, len(shape) - 1)


def column_offsets(shape):
    lane = lanes_of(shape)
    return jnp.where(lane < 192, lane, lane - 256)


def shifted_stack(x, spacing, width):
    return jnp.concatenate(
        [
            pltpu.roll(x, spacing, 1)[:, :width],
            x[:, :width],
            pltpu.roll(x, 256 - spacing, 1)[:, :width],
        ],
        axis=0,
    )


def tap_products(w, source, target, count, group, spacing, width):
    def body(g, carry):
        stack = jnp.concatenate(
            [shifted_stack(source[g * group + t], spacing, width) for t in range(group)], axis=1
        )
        product = jnp.dot(w[...], stack, preferred_element_type=F32)
        for t in range(group):
            target[g * group + t, :, 0:width] = product[:, t * width : (t + 1) * width]
        return carry

    lax.fori_loop(0, count // group, body, 0)


def tap_sum(target, i, spacing, width):
    return (
        target[i, 0:64, 0:width]
        + target[i + spacing, 64:128, 0:width]
        + target[i + 2 * spacing, 128:192, 0:width]
    )


def prepare_kernel(prior, rows_out, left_out, right_out):
    for q in range(4):
        rows_out[16 * q : 16 * q + 16] = jnp.swapaxes(prior[:, 16 * q : 16 * q + 16, :], 0, 1)
    part = lanes_of((64, 128)) // 16

    def body(q, carry):
        left = rows_out[8 * q]
        right = pltpu.roll(left, 16, 1)
        for k in range(1, 8):
            x = rows_out[8 * q + k]
            left = jnp.where(part == k, pltpu.roll(x, 16 * k, 1), left)
            right = jnp.where(part == k, pltpu.roll(x, (16 * k + 16) % 128, 1), right)
        left_out[q] = left
        right_out[q] = right
        return carry

    lax.fori_loop(0, 8, body, 0)


def prepare(prior):
    return pl.pallas_call(
        prepare_kernel,
        out_shape=(
            jax.ShapeDtypeStruct((TR, 64, TC), BF),
            jax.ShapeDtypeStruct((8, 64, TC), BF),
            jax.ShapeDtypeStruct((8, 64, TC), BF),
        ),
        in_specs=[vmem],
        out_specs=(vmem, vmem, vmem),
        compiler_params=pltpu.CompilerParams(vmem_limit_bytes=VMEM_BYTES),
    )(prior)


def exchange_kernel(feats, tile, left, right, rows, rim_left, rim_right, gathered,
                    send, recv, send_a, recv_a, send_b, recv_b, own):
    r, c = lax.axis_index("row"), lax.axis_index("col")
    up, down = lax.rem(r + ROWS - 1, ROWS), lax.rem(r + 1, ROWS)
    west, east = lax.rem(c + COLS - 1, COLS), lax.rem(c + 1, COLS)
    barrier = pltpu.get_barrier_semaphore()
    for d in range(1, COLS):
        pl.semaphore_signal(
            barrier, 1, device_id=(r, lax.rem(c + d, COLS)), device_id_type=MESH
        )
    for d in range(1, ROWS):
        pl.semaphore_signal(
            barrier, 1, device_id=(lax.rem(r + d, ROWS), c), device_id_type=MESH
        )
    for a in (up, down):
        for b in (west, east):
            pl.semaphore_signal(barrier, 1, device_id=(a, b), device_id_type=MESH)
    pl.semaphore_wait(barrier, COLS - 1 + ROWS - 1 + 4)

    def copy(source, target, out_sem, in_sem, to):
        return pltpu.make_async_remote_copy(
            src_ref=source,
            dst_ref=target,
            send_sem=out_sem,
            recv_sem=in_sem,
            device_id=to,
            device_id_type=MESH,
        )

    place = r * COLS + c
    mine = pltpu.make_async_copy(feats, gathered.at[place], own)
    mine.start()
    first = [
        copy(feats, gathered.at[place], send_a.at[d], recv_a.at[d], (r, lax.rem(c + d, COLS)))
        for d in range(1, COLS)
    ]
    for x in first:
        x.start()
    rims = [
        (right, rim_left.at[pl.ds(2, 8)], (r, east)),
        (left, rim_right.at[pl.ds(2, 8)], (r, west)),
        (tile.at[pl.ds(54, 10)], rows.at[0], (down, c)),
        (tile.at[pl.ds(0, 10)], rows.at[1], (up, c)),
        (right.at[pl.ds(6, 2)], rim_left.at[pl.ds(0, 2)], (down, east)),
        (right.at[pl.ds(0, 2)], rim_left.at[pl.ds(10, 2)], (up, east)),
        (left.at[pl.ds(6, 2)], rim_right.at[pl.ds(0, 2)], (down, west)),
        (left.at[pl.ds(0, 2)], rim_right.at[pl.ds(10, 2)], (up, west)),
    ]
    rims = [copy(s, t, send.at[k], recv.at[k], to) for k, (s, t, to) in enumerate(rims)]
    for x in rims:
        x.start()
    mine.wait()
    for x in first:
        x.wait_recv()
    block = gathered.at[pl.ds(r * COLS, COLS)]
    second = [
        copy(block, block, send_b.at[d], recv_b.at[d], (lax.rem(r + d, ROWS), c))
        for d in range(1, ROWS)
    ]
    for x in second:
        x.start()
    for x in first:
        x.wait_send()
    for x in rims:
        x.wait()
    for x in second:
        x.wait()


def exchange(feats, tile, left, right):
    return pl.pallas_call(
        exchange_kernel,
        out_shape=(
            jax.ShapeDtypeStruct((2, 10, 64, TC), BF),
            jax.ShapeDtypeStruct((12, 64, TC), BF),
            jax.ShapeDtypeStruct((12, 64, TC), BF),
            jax.ShapeDtypeStruct((ROWS * COLS, 8, TC), BF),
        ),
        in_specs=[anywhere] * 4,
        out_specs=(anywhere,) * 4,
        scratch_shapes=[
            pltpu.SemaphoreType.DMA((8,)),
            pltpu.SemaphoreType.DMA((8,)),
            pltpu.SemaphoreType.DMA((COLS,)),
            pltpu.SemaphoreType.DMA((COLS,)),
            pltpu.SemaphoreType.DMA((ROWS,)),
            pltpu.SemaphoreType.DMA((ROWS,)),
            pltpu.SemaphoreType.DMA,
        ],
        compiler_params=pltpu.CompilerParams(collective_id=1, has_side_effects=True),
    )(feats, tile, left, right)


def chosen_bins(gathered, first, ring):
    lanes = 256 if ring else 128
    shape = (SIDE, lanes)
    wanted = first + (column_offsets(shape) if ring else lanes_of(shape))
    picked = lax.broadcasted_iota(jnp.int32, shape, 0) == wanted
    return lax.dot_general(
        gathered[...],
        jnp.where(picked, 1.0, 0.0).astype(BF),
        (((0,), (0,)), ((), ())),
        preferred_element_type=F32,
    )


def coarse_kernel(place, tile, rows, rim_left, rim_right, gathered, w1, w2, w3, bias,
                  map_out, pieces, edges, x, taps, hidden, fr, fc):
    r, c = place()
    row0, col0 = r * TR, c * TC
    fr[...] = chosen_bins(gathered, row0 - 16, False)[0:64]
    fc[...] = chosen_bins(gathered, col0, True)[0:64]
    cols = col0 + column_offsets((64, 256))
    in_cols = (cols >= 0) & (cols < SIDE)
    low_half = lanes_of((64, 128)) < 64

    def pair_row(q, k, at, body):
        shift = pltpu.roll(fr[...], lax.rem(256 - 8 * q, 128), 1)
        rim = jnp.where(
            low_half,
            pltpu.roll(rim_right[q], (128 - 16 * k) % 128, 1),
            pltpu.roll(rim_left[q], 112 - 16 * k, 1),
        )
        prior = jnp.concatenate([body, rim], axis=1).astype(F32)
        value = prior + (fc[...] + shift[:, k : k + 1])
        grow = row0 + 8 * q + k - 16
        inside = in_cols & (grow >= 0) & (grow < SIDE)
        x[at] = jnp.where(inside, value, 0.0).astype(BF)

    for k in range(10):
        row = k - 10
        pair_row((row + 16) // 8, row % 8, k, rows[0, k])
        row = 64 + k
        pair_row((row + 16) // 8, row % 8, 74 + k, rows[1, k])

    def own_rows(g, carry):
        for k in range(8):
            pair_row(g + 2, k, 8 * g + k + 10, tile[8 * g + k])
        return carry

    lax.fori_loop(0, 8, own_rows, 0)
    tap_products(w1, x, taps, 84, 12, 2, 256)

    def hidden_row(i, carry):
        for t in range(4):
            at = 4 * i + t
            grow = row0 + at - 8
            value = jnp.maximum(tap_sum(taps, at, 2, 256) + bias[0], 0.0)
            inside = in_cols & (grow >= 0) & (grow < SIDE)
            hidden[at] = jnp.where(inside, value, 0.0).astype(BF)
        return carry

    lax.fori_loop(0, 20, hidden_row, 0)
    tap_products(w2, hidden, taps, 80, 10, 4, 256)
    half_c, half_r = lax.rem(c, COLS // 2) * TC, lax.rem(r, ROWS // 2) * TR
    cols_q = half_c + column_offsets((64, 256))
    in_quarter = (cols_q >= 0) & (cols_q < SIDE // 2)

    def map_row(i, carry):
        for t in range(4):
            at = 4 * i + t
            qrow = half_r + at - 4
            value = jnp.maximum(tap_sum(taps, at, 4, 256) + bias[1], 0.0)
            inside = in_quarter & (qrow >= 0) & (qrow < SIDE // 2)
            x[at] = jnp.where(inside, value, 0.0).astype(BF)
        return carry

    lax.fori_loop(0, 18, map_row, 0)
    for q in range(4):
        map_out[:, 16 * q : 16 * q + 16, :] = jnp.swapaxes(
            x[4 + 16 * q : 20 + 16 * q, :, 0:128], 0, 1
        )
    tap_products(w3, x, taps, 72, 12, 4, 128)
    part = lanes_of((64, 128)) // 8

    def pack(g, carry):
        t, half = g // 2, lax.rem(g, 2)
        found = [None] * 4
        previous = None
        for k in range(16):
            v = tap_sum(taps, 16 * g + k, 4, 128).astype(BF)
            for n, start in enumerate((0, 56, 64, 120)):
                moved = pltpu.roll(v, (8 * k - start) % 128, 1)
                found[n] = moved if k == 0 else jnp.where(part == k, moved, found[n])
            if k % 2 == 0:
                previous = v
            else:
                at = 1 + 8 * half + k // 2
                pieces[t, at] = jnp.where(low_half, previous, pltpu.roll(v, 64, 1))
                pieces[2 + t, at] = jnp.where(low_half, pltpu.roll(previous, 64, 1), v)
        edges[t, half] = found[0]
        pieces[2 + t, 17 * half] = found[1]
        pieces[t, 17 * half] = found[2]
        edges[2 + t, half] = found[3]
        return carry

    lax.fori_loop(0, 4, pack, 0)


def mesh_place():
    return lax.axis_index("row"), lax.axis_index("col")


def coarse(place, tile, rows, rim_left, rim_right, gathered, w1, w2, w3, bias):
    return pl.pallas_call(
        functools.partial(coarse_kernel, place),
        out_shape=(
            jax.ShapeDtypeStruct((64, TR, TC), BF),
            jax.ShapeDtypeStruct((4, 18, 64, TC), BF),
            jax.ShapeDtypeStruct((4, 2, 64, TC), BF),
        ),
        in_specs=[vmem] * 9,
        out_specs=(vmem,) * 3,
        scratch_shapes=[
            pltpu.VMEM((84, 64, 256), BF),
            pltpu.VMEM((84, 192, 256), F32),
            pltpu.VMEM((80, 64, 256), BF),
            pltpu.VMEM((64, 128), F32),
            pltpu.VMEM((64, 256), F32),
        ],
        compiler_params=pltpu.CompilerParams(vmem_limit_bytes=VMEM_BYTES),
    )(tile, rows, rim_left, rim_right, gathered, w1, w2, w3, bias)


def move_kernel(half, pieces, edges, got, outer, top, top_outer, bottom, bottom_outer,
                send, recv, send_o, recv_o, send_n, recv_n, own, own_o):
    r, c = lax.axis_index("row"), lax.axis_index("col")
    base_r, base_c = half * (ROWS // 2), half * (COLS // 2)
    up, down = lax.rem(r + ROWS - 1, ROWS), lax.rem(r + 1, ROWS)
    tile_c = c // 2
    other_c = jnp.where(lax.rem(c, 2) == 0, lax.rem(tile_c + 3, 4), lax.rem(tile_c + 1, 4))
    from_r, from_c, from_o = base_r + r // 2, base_c + tile_c, base_c + other_c
    remote_main = (from_r != r) | (from_c != c)
    remote_outer = (from_r != r) | (from_o != c)
    is_source = (r >= base_r) & (r < base_r + ROWS // 2) & (c >= base_c) & (c < base_c + COLS // 2)
    local_r, local_c = r - base_r, c - base_c
    mains = [(2 * local_r + t, 2 * local_c + h) for h in range(2) for t in range(2)]
    outers = [(2 * local_r + t, 2 * lax.rem(local_c + 3, 4) + 1) for t in range(2)] + [
        (2 * local_r + t, 2 * lax.rem(local_c + 1, 4)) for t in range(2)
    ]

    def away(to):
        return (to[0] != r) | (to[1] != c)

    barrier = pltpu.get_barrier_semaphore()

    def greet(to):
        pl.semaphore_signal(barrier, 1, device_id=to, device_id_type=MESH)

    greet((up, c))
    greet((down, c))
    pl.when(remote_main)(lambda: greet((from_r, from_c)))
    pl.when(remote_outer)(lambda: greet((from_r, from_o)))
    for to in mains + outers:
        pl.when(is_source & away(to))(functools.partial(greet, to))
    peers = 2 + jnp.where(remote_main, 1, 0) + jnp.where(remote_outer, 1, 0)
    for to in mains + outers:
        peers = peers + jnp.where(is_source & away(to), 1, 0)
    pl.semaphore_wait(barrier, peers)

    def copy(source, target, out_sem, in_sem, to):
        return pltpu.make_async_remote_copy(
            src_ref=source,
            dst_ref=target,
            send_sem=out_sem,
            recv_sem=in_sem,
            device_id=to,
            device_id_type=MESH,
        )

    sends = [
        (copy(pieces.at[k], got, send.at[k], recv, to), to) for k, to in enumerate(mains)
    ] + [
        (copy(edges.at[k], outer, send_o.at[k], recv_o, to), to) for k, to in enumerate(outers)
    ]
    stay = [
        (pltpu.make_async_copy(pieces.at[k], got, own), to) for k, to in enumerate(mains)
    ] + [
        (pltpu.make_async_copy(edges.at[k], outer, own_o), to) for k, to in enumerate(outers)
    ]
    for (x, to), (y, _) in zip(sends, stay, strict=True):
        pl.when(is_source & away(to))(x.start)
        pl.when(is_source & jnp.logical_not(away(to)))(y.start)
    main_in = copy(pieces.at[0], got, send.at[0], recv, (up, c))
    outer_in = copy(edges.at[0], outer, send_o.at[0], recv_o, (up, c))
    pl.when(remote_main)(main_in.wait_recv)
    pl.when(jnp.logical_not(remote_main))(stay[0][0].wait)
    pl.when(remote_outer)(outer_in.wait_recv)
    pl.when(jnp.logical_not(remote_outer))(stay[4][0].wait)
    rims = [
        (got.at[pl.ds(13, 5)], top, (down, c)),
        (got.at[pl.ds(0, 5)], bottom, (up, c)),
        (outer.at[pl.ds(1, 1)], top_outer, (down, c)),
        (outer.at[pl.ds(0, 1)], bottom_outer, (up, c)),
    ]
    rims = [copy(s, t, send_n.at[k], recv_n.at[k], to) for k, (s, t, to) in enumerate(rims)]
    for x in rims:
        x.start()
    for x, to in sends:
        pl.when(is_source & away(to))(x.wait_send)
    for x in rims:
        x.wait()


def move(half, pieces, edges):
    return pl.pallas_call(
        functools.partial(move_kernel, half),
        out_shape=(
            jax.ShapeDtypeStruct((18, 64, TC), BF),
            jax.ShapeDtypeStruct((2, 64, TC), BF),
            jax.ShapeDtypeStruct((5, 64, TC), BF),
            jax.ShapeDtypeStruct((1, 64, TC), BF),
            jax.ShapeDtypeStruct((5, 64, TC), BF),
            jax.ShapeDtypeStruct((1, 64, TC), BF),
        ),
        in_specs=[anywhere] * 2,
        out_specs=(anywhere,) * 6,
        scratch_shapes=[
            pltpu.SemaphoreType.DMA((4,)),
            pltpu.SemaphoreType.DMA,
            pltpu.SemaphoreType.DMA((4,)),
            pltpu.SemaphoreType.DMA,
            pltpu.SemaphoreType.DMA((4,)),
            pltpu.SemaphoreType.DMA((4,)),
            pltpu.SemaphoreType.DMA,
            pltpu.SemaphoreType.DMA,
        ],
        compiler_params=pltpu.CompilerParams(collective_id=2 + half, has_side_effects=True),
    )(pieces, edges)


def spread_tables():
    lane = np.arange(128)
    source = np.arange(128)[:, None]
    main = np.stack([source == 64 * k + lane[None] // 2 for k in range(2)])
    rim = np.zeros((256, 16, 128), bool)
    for k in range(16):
        rim[:128, k] = (source == 8 * k + lane[None] // 2) & (lane[None] < 16)
        rim[128:, k] = (source == 8 * k + (lane[None] - 112) // 2) & (lane[None] >= 112)
    return main.astype(np.float32), rim.reshape(256, 2048).astype(np.float32)


def refine_kernel(place, got, outer, top, top_outer, bottom, bottom_outer, gathered,
                  wq, wp, w4, bias, main_table, rim_table,
                  out, wide, hidden, taps, row_terms, row_part):
    r, c = place()
    row0, col0 = r * TR, c * TC
    fc = chosen_bins(gathered, col0, True)[64:128].astype(BF)
    q = jnp.dot(wq[...], shifted_stack(fc, 8, 256), preferred_element_type=F32)
    base = q[64:128] + bias[0]
    row_terms[0] = base + q[0:64] + q[128:192]
    row_terms[1] = base + q[128:192]
    row_terms[2] = base + q[0:64]
    fr = chosen_bins(gathered, row0 - 24, False)[64:128].astype(BF)
    stack = jnp.concatenate([pltpu.roll(fr, 8, 1), fr, pltpu.roll(fr, 120, 1)], axis=0)
    p = jnp.dot(wp[...], stack, preferred_element_type=F32)
    row_part[0] = p[0:64] + p[64:128] + p[128:192]
    row_part[1] = p[64:128] + jnp.where(c == 0, p[128:192], p[0:64])
    cols = col0 + column_offsets((64, 256))
    in_cols = (cols >= 0) & (cols < SIDE)
    at_edge = (cols < 8) | (cols >= SIDE - 8)

    def spread_main(source, first, count, at):
        for k in range(2):
            value = jnp.dot(
                source[first : first + count].reshape(count * 64, 128),
                main_table[k],
                preferred_element_type=F32,
            )
            wide[at : at + count, k, :, 0:128] = value.reshape(count, 64, 128).astype(BF)

    spread_main(top, 0, 4, 0)
    spread_main(got, 1, 16, 4)
    spread_main(bottom, 1, 4, 20)
    inner_right = lax.rem(c, 2) == 0

    def spread_rim(inside, outside, low, high, first):
        both = jnp.concatenate(
            [
                jnp.where(inner_right, inside, outside),
                jnp.where(inner_right, outside, inside),
            ],
            axis=1,
        )
        value = jnp.dot(
            both, rim_table[:, 128 * low : 128 * high], preferred_element_type=F32
        ).astype(BF)
        for k in range(high - low):
            row = first + k
            wide[row // 2, row % 2, :, 128:256] = value[:, 128 * k : 128 * k + 128]

    spread_rim(top[4], top_outer[0], 8, 16, 0)
    spread_rim(got[0], outer[0], 0, 16, 8)
    spread_rim(got[17], outer[1], 0, 16, 24)
    spread_rim(bottom[0], bottom_outer[0], 0, 8, 40)

    def hidden_rows(g, carry):
        grow0 = row0 + 8 * g - 16
        inside = in_cols & (grow0 >= 0) & (grow0 < SIDE)
        variant = jnp.where(grow0 == 0, 1, jnp.where(grow0 == SIDE - 8, 2, 0))
        shift = lax.rem(256 - 8 * g - 8, 128)
        everywhere = pltpu.roll(row_part[0], shift, 1)
        edge = pltpu.roll(row_part[1], shift, 1)
        terms = row_terms[variant]
        for k in range(8):
            row = jnp.where(at_edge, edge[:, k : k + 1], everywhere[:, k : k + 1])
            value = wide[2 * g + k // 4, (k // 2) % 2].astype(F32) + (terms + row)
            hidden[8 * g + k] = jnp.where(inside, jnp.maximum(value, 0.0), 0.0).astype(BF)
        return carry

    lax.fori_loop(0, 12, hidden_rows, 0)
    tap_products(w4, hidden, taps, 96, 12, 16, 128)

    for g in range(4):
        value = jnp.stack(
            [
                jnp.maximum(tap_sum(taps, 16 * g + k, 16, 128) + bias[1, :, 0:128], 0.0).astype(BF)
                for k in range(16)
            ]
        )
        out[:, 16 * g : 16 * g + 16, :] = jnp.swapaxes(value, 0, 1)


def refine(place, got, outer, top, top_outer, bottom, bottom_outer, gathered, wq, wp, w4, bias):
    main_table, rim_table = spread_tables()
    return pl.pallas_call(
        functools.partial(refine_kernel, place),
        out_shape=jax.ShapeDtypeStruct((64, TR, TC), BF),
        in_specs=[vmem] * 13,
        out_specs=vmem,
        scratch_shapes=[
            pltpu.VMEM((24, 2, 64, 256), BF),
            pltpu.VMEM((96, 64, 256), BF),
            pltpu.VMEM((96, 192, 128), F32),
            pltpu.VMEM((3, 64, 256), F32),
            pltpu.VMEM((2, 64, 128), F32),
        ],
        compiler_params=pltpu.CompilerParams(vmem_limit_bytes=VMEM_BYTES),
    )(got, outer, top, top_outer, bottom, bottom_outer, gathered, wq, wp, w4, bias,
      jnp.asarray(main_table, BF), jnp.asarray(rim_table, BF))


def weight_forms(coarse_weights, coarse_bias, refine_first, refine_second, refine_bias):
    w1 = coarse_weights[0].reshape(192, 192)
    w2 = coarse_weights[1].reshape(192, 192)
    first = refine_first.reshape(3, 64, 3, 128)
    w3 = first[..., :64].reshape(192, 192)
    fine = first[..., 64:]
    wq = fine.reshape(192, 192)
    wp = fine.transpose(2, 1, 0, 3).reshape(192, 192)
    w4 = refine_second.reshape(192, 192)
    b12 = jnp.broadcast_to(coarse_bias[:, :, None], (2, 64, 256))
    b34 = jnp.broadcast_to(refine_bias[:, :, None], (2, 64, 256))
    return w1, w2, w3, wq, wp, w4, b12, b34


def per_device(coarse_feats, fine_feats, pair_prior, zoom_start, coarse_weights, coarse_bias,
               refine_first, refine_second, refine_bias):
    w1, w2, w3, wq, wp, w4, b12, b34 = weight_forms(
        coarse_weights, coarse_bias, refine_first, refine_second, refine_bias
    )
    feats = jnp.concatenate([coarse_feats, fine_feats], axis=0).T
    tile, left, right = prepare(pair_prior)
    rows, rim_left, rim_right, gathered = exchange(feats, tile, left, right)
    gathered = gathered.reshape(SIDE, 128)
    coarse_map, pieces, edges = coarse(
        mesh_place, tile, rows, rim_left, rim_right, gathered, w1, w2, w3, b12
    )
    moved = lax.cond(
        zoom_start[0] == 0,
        functools.partial(move, 0),
        functools.partial(move, 1),
        pieces,
        edges,
    )
    refined = refine(mesh_place, *moved, gathered, wq, wp, w4, b34)
    return coarse_map, refined


def solution(mesh):
    return jax.shard_map(
        per_device,
        mesh=mesh,
        in_specs=(
            P(None, ("row", "col")),
            P(None, ("row", "col")),
            P(None, "row", "col"),
            P(),
            P(),
            P(),
            P(),
            P(),
            P(),
        ),
        out_specs=(P(None, "row", "col"), P(None, "row", "col")),
        check_vma=False,
    )
```

```python
import functools

import jax
import jax.numpy as jnp
import numpy as np
from jax import lax
from jax.experimental import pallas as pl
from jax.experimental.pallas import tpu as pltpu
from jax.sharding import PartitionSpec as P

BF = jnp.bfloat16
F32 = jnp.float32
MESH = pl.DeviceIdType.MESH
VMEM_BYTES = 58 << 20
SIDE = 1024
ROWS, COLS = 16, 8
TR, TC = 64, 128

vmem = pl.BlockSpec(memory_space=pltpu.VMEM)
anywhere = pl.BlockSpec(memory_space=pl.ANY)


def lanes_of(shape):
    return lax.broadcasted_iota(jnp.int32, shape, len(shape) - 1)


def column_offsets(shape):
    lane = lanes_of(shape)
    return jnp.where(lane < 192, lane, lane - 256)


def shifted_stack(x, spacing, width):
    return jnp.concatenate(
        [
            pltpu.roll(x, spacing, 1)[:, :width],
            x[:, :width],
            pltpu.roll(x, 256 - spacing, 1)[:, :width],
        ],
        axis=0,
    )


def tap_products(w, source, first, target, into, count, group, spacing, width):
    for g in range(count // group):
        base = first + g * group
        stack = jnp.concatenate(
            [shifted_stack(source[base + t], spacing, width) for t in range(group)], axis=1
        )
        product = jnp.dot(w, stack, preferred_element_type=F32)
        for t in range(group):
            target[into + g * group + t] = product[:, t * width : (t + 1) * width]


def carry_taps(target, spacing):
    last = target.shape[0] - 2 * spacing
    for t in range(2 * spacing):
        target[t, 0:64] = target[last + t, 0:64]
        if t >= spacing:
            target[t, 64:128] = target[last + t, 64:128]


def tap_sum(target, i, spacing, width):
    return (
        target[i, 0:64, 0:width]
        + target[i + spacing, 64:128, 0:width]
        + target[i + 2 * spacing, 128:192, 0:width]
    )


def bias_columns(bias, layer, width):
    row = jnp.broadcast_to(bias[layer : layer + 1, :], (128, 64))
    column = jnp.transpose(row)
    return column if width == 128 else jnp.concatenate([column, column], axis=1)


def halves_joined(a, b, c, upper):
    low = lanes_of(a.shape) < 64
    if upper:
        first = jnp.where(low, pltpu.roll(a, 64, 1), b)
        return jnp.concatenate([first, pltpu.roll(c, 64, 1)[:, :64]], axis=1)
    first = jnp.where(low, a, pltpu.roll(b, 64, 1))
    return jnp.concatenate([first, c[:, :64]], axis=1)


def gather_kernel(coarse_feats, fine_feats, prior, tile, rows, rim_left, rim_right, gathered,
                  feats, left, right, send, recv, send_a, recv_a, send_b, recv_b, own):
    r, c = lax.axis_index("row"), lax.axis_index("col")
    up, down = lax.rem(r + ROWS - 1, ROWS), lax.rem(r + 1, ROWS)
    west, east = lax.rem(c + COLS - 1, COLS), lax.rem(c + 1, COLS)
    has_up, has_down, has_west, has_east = r > 0, r < ROWS - 1, c > 0, c < COLS - 1
    barrier = pltpu.get_barrier_semaphore()

    def greet(to):
        pl.semaphore_signal(barrier, 1, device_id=to, device_id_type=MESH)

    for d in range(1, COLS):
        greet((r, lax.rem(c + d, COLS)))
    for d in range(1, ROWS):
        greet((lax.rem(r + d, ROWS), c))
    peers = COLS - 1 + ROWS - 1
    for a, has_a in ((up, has_up), (down, has_down)):
        for b, has_b in ((west, has_west), (east, has_east)):
            pl.when(has_a & has_b)(functools.partial(greet, (a, b)))
            peers = peers + jnp.where(has_a & has_b, 1, 0)

    both = jnp.concatenate([coarse_feats[...], fine_feats[...]], axis=0).astype(F32)
    feats[...] = jnp.transpose(both).astype(BF)
    for q in range(4):
        tile[16 * q : 16 * q + 16] = jnp.swapaxes(prior[:, 16 * q : 16 * q + 16, :], 0, 1)
    part = lanes_of((64, 128)) // 16

    def pack(q, carry):
        low = tile[8 * q]
        high = pltpu.roll(low, 16, 1)
        for k in range(1, 8):
            x = tile[8 * q + k]
            low = jnp.where(part == k, pltpu.roll(x, 16 * k, 1), low)
            high = jnp.where(part == k, pltpu.roll(x, (16 * k + 16) % 128, 1), high)
        left[q] = low
        right[q] = high
        return carry

    def copy(source, target, out_sem, in_sem, to):
        return pltpu.make_async_remote_copy(
            src_ref=source,
            dst_ref=target,
            send_sem=out_sem,
            recv_sem=in_sem,
            device_id=to,
            device_id_type=MESH,
        )

    pl.semaphore_wait(barrier, peers)
    place = r * COLS + c
    mine = pltpu.make_async_copy(feats, gathered.at[place], own)
    mine.start()
    first = [
        copy(feats, gathered.at[place], send_a.at[d], recv_a.at[d], (r, lax.rem(c + d, COLS)))
        for d in range(1, COLS)
    ]
    for x in first:
        x.start()
    lax.fori_loop(0, 8, pack, 0)
    rims = [
        (right, rim_left.at[pl.ds(2, 8)], (r, east), has_east, has_west),
        (left, rim_right.at[pl.ds(2, 8)], (r, west), has_west, has_east),
        (tile.at[pl.ds(54, 10)], rows.at[0], (down, c), has_down, has_up),
        (tile.at[pl.ds(0, 10)], rows.at[1], (up, c), has_up, has_down),
        (right.at[pl.ds(6, 2)], rim_left.at[pl.ds(0, 2)], (down, east),
         has_down & has_east, has_up & has_west),
        (right.at[pl.ds(0, 2)], rim_left.at[pl.ds(10, 2)], (up, east),
         has_up & has_east, has_down & has_west),
        (left.at[pl.ds(6, 2)], rim_right.at[pl.ds(0, 2)], (down, west),
         has_down & has_west, has_up & has_east),
        (left.at[pl.ds(0, 2)], rim_right.at[pl.ds(10, 2)], (up, west),
         has_up & has_west, has_down & has_east),
    ]
    rims = [
        (copy(s, t, send.at[k], recv.at[k], to), out, into)
        for k, (s, t, to, out, into) in enumerate(rims)
    ]
    for x, out, _ in rims:
        pl.when(out)(x.start)
    mine.wait()
    for x in first:
        x.wait_recv()
    block = gathered.at[pl.ds(r * COLS, COLS)]
    second = [
        copy(block, block, send_b.at[d], recv_b.at[d], (lax.rem(r + d, ROWS), c))
        for d in range(1, ROWS)
    ]
    for x in second:
        x.start()
    for x in first:
        x.wait_send()
    for x, out, into in rims:
        pl.when(out)(x.wait_send)
        pl.when(into)(x.wait_recv)
    for x in second:
        x.wait()


def gather(coarse_feats, fine_feats, prior):
    return pl.pallas_call(
        gather_kernel,
        out_shape=(
            jax.ShapeDtypeStruct((TR, 64, TC), BF),
            jax.ShapeDtypeStruct((2, 10, 64, TC), BF),
            jax.ShapeDtypeStruct((12, 64, TC), BF),
            jax.ShapeDtypeStruct((12, 64, TC), BF),
            jax.ShapeDtypeStruct((ROWS * COLS, 8, TC), BF),
        ),
        in_specs=[vmem] * 3,
        out_specs=(vmem,) + (anywhere,) * 4,
        scratch_shapes=[
            pltpu.VMEM((8, TC), BF),
            pltpu.VMEM((8, 64, TC), BF),
            pltpu.VMEM((8, 64, TC), BF),
            pltpu.SemaphoreType.DMA((8,)),
            pltpu.SemaphoreType.DMA((8,)),
            pltpu.SemaphoreType.DMA((COLS,)),
            pltpu.SemaphoreType.DMA((COLS,)),
            pltpu.SemaphoreType.DMA((ROWS,)),
            pltpu.SemaphoreType.DMA((ROWS,)),
            pltpu.SemaphoreType.DMA,
        ],
        compiler_params=pltpu.CompilerParams(
            collective_id=1, has_side_effects=True, vmem_limit_bytes=VMEM_BYTES
        ),
    )(coarse_feats, fine_feats, prior)


def chosen_bins(gathered, first, ring):
    lanes = 256 if ring else 128
    shape = (SIDE, lanes)
    wanted = first + (column_offsets(shape) if ring else lanes_of(shape))
    picked = lax.broadcasted_iota(jnp.int32, shape, 0) == wanted
    return lax.dot_general(
        gathered[...],
        jnp.where(picked, 1.0, 0.0).astype(BF),
        (((0,), (0,)), ((), ())),
        preferred_element_type=F32,
    )


def coarse_kernel(half, tile, rows, rim_left, rim_right, gathered, weights, first_refine, biases,
                  map_out, got, outer, top, top_outer, bottom, bottom_outer,
                  x, taps1, hidden, taps2, fields, taps3, w3, bias, fr, fc, pieces, edges,
                  send, recv, send_o, recv_o, send_n, recv_n, own, own_o):
    r, c = lax.axis_index("row"), lax.axis_index("col")
    base_r, base_c = half * (ROWS // 2), half * (COLS // 2)
    up, down = lax.rem(r + ROWS - 1, ROWS), lax.rem(r + 1, ROWS)
    tile_c = c // 2
    other_c = jnp.where(lax.rem(c, 2) == 0, lax.rem(tile_c + 3, 4), lax.rem(tile_c + 1, 4))
    from_r, from_c, from_o = base_r + r // 2, base_c + tile_c, base_c + other_c
    remote_main = (from_r != r) | (from_c != c)
    remote_outer = (from_r != r) | (from_o != c)
    is_source = (r >= base_r) & (r < base_r + ROWS // 2) & (c >= base_c) & (c < base_c + COLS // 2)
    local_r, local_c = r - base_r, c - base_c

    def main_to(t, h):
        return 2 * local_r + t, 2 * local_c + h

    def outer_to(t, side):
        if side == 0:
            return 2 * local_r + t, 2 * lax.rem(local_c + 3, 4) + 1
        return 2 * local_r + t, 2 * lax.rem(local_c + 1, 4)

    def away(to):
        return (to[0] != r) | (to[1] != c)

    barrier = pltpu.get_barrier_semaphore()

    def greet(to):
        pl.semaphore_signal(barrier, 1, device_id=to, device_id_type=MESH)

    greet((up, c))
    greet((down, c))
    pl.when(remote_main)(lambda: greet((from_r, from_c)))
    pl.when(remote_outer)(lambda: greet((from_r, from_o)))
    peers = 2 + jnp.where(remote_main, 1, 0) + jnp.where(remote_outer, 1, 0)
    for t in range(2):
        for k in range(2):
            for to in (main_to(t, k), outer_to(t, k)):
                pl.when(is_source & away(to))(functools.partial(greet, to))
                peers = peers + jnp.where(is_source & away(to), 1, 0)

    def copy(source, target, out_sem, in_sem, to):
        return pltpu.make_async_remote_copy(
            src_ref=source,
            dst_ref=target,
            send_sem=out_sem,
            recv_sem=in_sem,
            device_id=to,
            device_id_type=MESH,
        )

    def transfers(j):
        t, q = j // 2, lax.rem(j, 2)
        found = []
        for k in range(2):
            to = main_to(t, k)
            s, d = pieces.at[k, t, pl.ds(9 * q, 9)], got.at[pl.ds(9 * q, 9)]
            found.append(
                (copy(s, d, send.at[2 * j + k], recv.at[q], to),
                 pltpu.make_async_copy(s, d, own.at[q]), to)
            )
            to = outer_to(t, k)
            s, d = edges.at[k, t, pl.ds(q, 1)], outer.at[pl.ds(q, 1)]
            found.append(
                (copy(s, d, send_o.at[2 * j + k], recv_o.at[q], to),
                 pltpu.make_async_copy(s, d, own_o.at[q]), to)
            )
        return found

    w1 = weights[0].reshape(192, 192)
    w2 = weights[1].reshape(192, 192)
    joined = first_refine[...].reshape(192, 384)
    w3[...] = halves_joined(joined[:, 0:128], joined[:, 128:256], joined[:, 256:384], False)
    bias[0] = bias_columns(biases, 0, 256)
    bias[1] = bias_columns(biases, 1, 256)
    row0, col0 = r * TR, c * TC
    fr[...] = chosen_bins(gathered, row0 - 16, False)[0:64]
    fc[...] = chosen_bins(gathered, col0, True)[0:64]
    cols = col0 + column_offsets((64, 256))
    in_cols = (cols >= 0) & (cols < SIDE)
    half_c, half_r = lax.rem(c, COLS // 2) * TC, lax.rem(r, ROWS // 2) * TR
    cols_q = half_c + column_offsets((64, 256))
    in_quarter = (cols_q >= 0) & (cols_q < SIDE // 2)
    low_half = lanes_of((64, 128)) < 64
    part = lanes_of((64, 128)) // 8

    def pair_row(q, k, at, body, shift):
        rim = jnp.where(
            low_half,
            pltpu.roll(rim_right[q], (128 - 16 * k) % 128, 1),
            pltpu.roll(rim_left[q], 112 - 16 * k, 1),
        )
        prior = jnp.concatenate([body, rim], axis=1).astype(F32)
        value = prior + (fc[...] + shift[:, k : k + 1])
        grow = row0 + 8 * q + k - 16
        inside = in_cols & (grow >= 0) & (grow < SIDE)
        x[at] = jnp.where(inside, value, 0.0).astype(BF)

    def features_at(q):
        return pltpu.roll(fr[...], lax.rem(256 - 8 * q, 128), 1)

    def rim_rows(side):
        for k in range(10):
            row = 64 + k if side else k - 10
            q = (row + 16) // 8
            pair_row(q, row % 8, row + 10, rows[side, k], features_at(q))

    def own_rows(g):
        shift = features_at(g + 2)
        for k in range(8):
            pair_row(g + 2, k, 8 * g + k + 10, tile[8 * g + k], shift)

    def hidden_rows(first, taken, count):
        for t in range(count):
            at = first + t
            grow = row0 + at - 8
            value = jnp.maximum(tap_sum(taps1, taken + t, 2, 256) + bias[0], 0.0)
            inside = in_cols & (grow >= 0) & (grow < SIDE)
            hidden[at] = jnp.where(inside, value, 0.0).astype(BF)

    def field_rows(first, taken, count):
        for t in range(count):
            at = first + t
            qrow = half_r + at - 4
            value = jnp.maximum(tap_sum(taps2, taken + t, 4, 256) + bias[1], 0.0)
            inside = in_quarter & (qrow >= 0) & (qrow < SIDE // 2)
            fields[at] = jnp.where(inside, value, 0.0).astype(BF)

    def pack(j):
        t, q = j // 2, lax.rem(j, 2)
        found = [None] * 4
        previous = None
        for k in range(16):
            v = tap_sum(taps3, k, 4, 128).astype(BF)
            for n, start in enumerate((0, 56, 64, 120)):
                moved = pltpu.roll(v, (8 * k - start) % 128, 1)
                found[n] = moved if k == 0 else jnp.where(part == k, moved, found[n])
            if k % 2 == 0:
                previous = v
            else:
                at = 1 + 8 * q + k // 2
                pieces[0, t, at] = jnp.where(low_half, previous, pltpu.roll(v, 64, 1))
                pieces[1, t, at] = jnp.where(low_half, pltpu.roll(previous, 64, 1), v)
        edges[0, t, q] = found[0]
        pieces[1, t, 17 * q] = found[1]
        pieces[0, t, 17 * q] = found[2]
        edges[1, t, q] = found[3]

    rim_rows(0)

    def early_rows(g, carry):
        own_rows(g)
        return carry

    lax.fori_loop(0, 4, early_rows, 0)
    tap_products(w1, x, 0, taps1, 0, 20, 10, 2, 256)
    hidden_rows(0, 0, 16)
    tap_products(w2, hidden, 0, taps2, 8, 16, 8, 4, 256)
    field_rows(0, 8, 8)
    tap_products(w3[...], fields, 0, taps3, 16, 8, 8, 4, 128)
    pl.semaphore_wait(barrier, peers)

    def chunk(j, carry):
        @pl.when((j == 1) | (j == 2))
        def _():
            own_rows(2 * j + 2)
            own_rows(2 * j + 3)

        pl.when(j == 3)(lambda: rim_rows(1))
        carry_taps(taps1, 2)
        carry_taps(taps2, 4)
        carry_taps(taps3, 4)
        tap_products(w1, x, 20 + 16 * j, taps1, 4, 16, 8, 2, 256)
        hidden_rows(16 + 16 * j, 0, 16)
        tap_products(w2, hidden, 16 + 16 * j, taps2, 8, 16, 8, 4, 256)
        field_rows(8 + 16 * j, 0, 16)
        tap_products(w3[...], fields, 8 + 16 * j, taps3, 8, 16, 8, 4, 128)
        pack(j)
        for out, stay, to in transfers(j):
            pl.when(is_source & away(to))(out.start)
            pl.when(is_source & jnp.logical_not(away(to)))(stay.start)
        return carry

    lax.fori_loop(0, 4, chunk, 0)
    for q in range(4):
        map_out[:, 16 * q : 16 * q + 16, :] = jnp.swapaxes(
            fields[4 + 16 * q : 20 + 16 * q, :, 0:128], 0, 1
        )
    for q in range(2):
        (main_in, main_own, _), (outer_in, outer_own, _) = transfers(q)[:2]
        pl.when(remote_main)(main_in.wait_recv)
        pl.when(jnp.logical_not(remote_main))(main_own.wait)
        pl.when(remote_outer)(outer_in.wait_recv)
        pl.when(jnp.logical_not(remote_outer))(outer_own.wait)
    rims = [
        (got.at[pl.ds(13, 5)], top, (down, c)),
        (got.at[pl.ds(0, 5)], bottom, (up, c)),
        (outer.at[pl.ds(1, 1)], top_outer, (down, c)),
        (outer.at[pl.ds(0, 1)], bottom_outer, (up, c)),
    ]
    rims = [copy(s, t, send_n.at[k], recv_n.at[k], to) for k, (s, t, to) in enumerate(rims)]
    for y in rims:
        y.start()
    for j in range(4):
        for out, _, to in transfers(j):
            pl.when(is_source & away(to))(out.wait_send)
    for y in rims:
        y.wait()


def coarse(half, tile, rows, rim_left, rim_right, gathered, weights, first_refine, biases):
    return pl.pallas_call(
        functools.partial(coarse_kernel, half),
        out_shape=(
            jax.ShapeDtypeStruct((64, TR, TC), BF),
            jax.ShapeDtypeStruct((18, 64, TC), BF),
            jax.ShapeDtypeStruct((2, 64, TC), BF),
            jax.ShapeDtypeStruct((5, 64, TC), BF),
            jax.ShapeDtypeStruct((1, 64, TC), BF),
            jax.ShapeDtypeStruct((5, 64, TC), BF),
            jax.ShapeDtypeStruct((1, 64, TC), BF),
        ),
        in_specs=[vmem] * 8,
        out_specs=(vmem,) + (anywhere,) * 6,
        scratch_shapes=[
            pltpu.VMEM((84, 64, 256), BF),
            pltpu.VMEM((20, 192, 256), F32),
            pltpu.VMEM((80, 64, 256), BF),
            pltpu.VMEM((24, 192, 256), F32),
            pltpu.VMEM((72, 64, 256), BF),
            pltpu.VMEM((24, 192, 128), F32),
            pltpu.VMEM((192, 192), BF),
            pltpu.VMEM((2, 64, 256), F32),
            pltpu.VMEM((64, 128), F32),
            pltpu.VMEM((64, 256), F32),
            pltpu.VMEM((2, 2, 18, 64, 128), BF),
            pltpu.VMEM((2, 2, 2, 64, 128), BF),
            pltpu.SemaphoreType.DMA((8,)),
            pltpu.SemaphoreType.DMA((2,)),
            pltpu.SemaphoreType.DMA((8,)),
            pltpu.SemaphoreType.DMA((2,)),
            pltpu.SemaphoreType.DMA((4,)),
            pltpu.SemaphoreType.DMA((4,)),
            pltpu.SemaphoreType.DMA((2,)),
            pltpu.SemaphoreType.DMA((2,)),
        ],
        compiler_params=pltpu.CompilerParams(
            collective_id=2 + half, has_side_effects=True, vmem_limit_bytes=VMEM_BYTES
        ),
    )(tile, rows, rim_left, rim_right, gathered, weights, first_refine, biases)


def mesh_place():
    return lax.axis_index("row"), lax.axis_index("col")


def spread_tables():
    lane = np.arange(128)
    source = np.arange(128)[:, None]
    main = np.stack([source == 64 * k + lane[None] // 2 for k in range(2)])
    rim = np.zeros((256, 16, 128), bool)
    for k in range(16):
        rim[:128, k] = (source == 8 * k + lane[None] // 2) & (lane[None] < 16)
        rim[128:, k] = (source == 8 * k + (lane[None] - 112) // 2) & (lane[None] >= 112)
    return main.astype(np.float32), rim.reshape(256, 2048).astype(np.float32)


def refine_kernel(place, got, outer, top, top_outer, bottom, bottom_outer, gathered,
                  first_refine, second_refine, biases, main_table, rim_table,
                  out, wide, hidden, taps, row_terms, row_part, bias):
    r, c = place()
    row0, col0 = r * TR, c * TC
    joined = first_refine[...].reshape(192, 384)
    wq = halves_joined(joined[:, 0:128], joined[:, 128:256], joined[:, 256:384], True)
    wp = jnp.concatenate(
        [
            halves_joined(*[first_refine[a, :, 128 * e : 128 * e + 128] for a in range(3)], True)
            for e in range(3)
        ],
        axis=0,
    )
    w4 = second_refine[...].reshape(192, 192)
    bias[...] = bias_columns(biases, 1, 128)
    fc = chosen_bins(gathered, col0, True)[64:128].astype(BF)
    q = jnp.dot(wq, shifted_stack(fc, 8, 256), preferred_element_type=F32)
    base = q[64:128] + bias_columns(biases, 0, 256)
    row_terms[0] = base + q[0:64] + q[128:192]
    row_terms[1] = base + q[128:192]
    row_terms[2] = base + q[0:64]
    fr = chosen_bins(gathered, row0 - 24, False)[64:128].astype(BF)
    stack = jnp.concatenate([pltpu.roll(fr, 8, 1), fr, pltpu.roll(fr, 120, 1)], axis=0)
    p = jnp.dot(wp, stack, preferred_element_type=F32)
    row_part[0] = p[0:64] + p[64:128] + p[128:192]
    row_part[1] = p[64:128] + jnp.where(c == 0, p[128:192], p[0:64])
    cols = col0 + column_offsets((64, 256))
    in_cols = (cols >= 0) & (cols < SIDE)
    at_edge = (cols < 8) | (cols >= SIDE - 8)

    def spread_main(source, first, count, at):
        for k in range(2):
            value = jnp.dot(
                source[first : first + count].reshape(count * 64, 128),
                main_table[k],
                preferred_element_type=F32,
            )
            wide[at : at + count, k, :, 0:128] = value.reshape(count, 64, 128).astype(BF)

    spread_main(top, 0, 4, 0)
    spread_main(got, 1, 16, 4)
    spread_main(bottom, 1, 4, 20)
    inner_right = lax.rem(c, 2) == 0

    def spread_rim(inside, outside, low, high, first):
        both = jnp.concatenate(
            [
                jnp.where(inner_right, inside, outside),
                jnp.where(inner_right, outside, inside),
            ],
            axis=1,
        )
        value = jnp.dot(
            both, rim_table[:, 128 * low : 128 * high], preferred_element_type=F32
        ).astype(BF)
        for k in range(high - low):
            row = first + k
            wide[row // 2, row % 2, :, 128:256] = value[:, 128 * k : 128 * k + 128]

    spread_rim(top[4], top_outer[0], 8, 16, 0)
    spread_rim(got[0], outer[0], 0, 16, 8)
    spread_rim(got[17], outer[1], 0, 16, 24)
    spread_rim(bottom[0], bottom_outer[0], 0, 8, 40)

    def hidden_rows(g, carry):
        grow0 = row0 + 8 * g - 16
        inside = in_cols & (grow0 >= 0) & (grow0 < SIDE)
        variant = jnp.where(grow0 == 0, 1, jnp.where(grow0 == SIDE - 8, 2, 0))
        shift = lax.rem(256 - 8 * g - 8, 128)
        everywhere = pltpu.roll(row_part[0], shift, 1)
        edge = pltpu.roll(row_part[1], shift, 1)
        terms = row_terms[variant]
        for k in range(8):
            row = jnp.where(at_edge, edge[:, k : k + 1], everywhere[:, k : k + 1])
            value = wide[2 * g + k // 4, (k // 2) % 2].astype(F32) + (terms + row)
            hidden[8 * g + k] = jnp.where(inside, jnp.maximum(value, 0.0), 0.0).astype(BF)
        return carry

    lax.fori_loop(0, 12, hidden_rows, 0)

    def last_products(g, carry):
        tap_products(w4, hidden, 16 * g, taps, 16 * g, 16, 8, 16, 128)
        return carry

    lax.fori_loop(0, 6, last_products, 0)

    for g in range(4):
        value = jnp.stack(
            [
                jnp.maximum(tap_sum(taps, 16 * g + k, 16, 128) + bias[...], 0.0).astype(BF)
                for k in range(16)
            ]
        )
        out[:, 16 * g : 16 * g + 16, :] = jnp.swapaxes(value, 0, 1)


def refine(place, got, outer, top, top_outer, bottom, bottom_outer, gathered,
           first_refine, second_refine, biases):
    main_table, rim_table = spread_tables()
    return pl.pallas_call(
        functools.partial(refine_kernel, place),
        out_shape=jax.ShapeDtypeStruct((64, TR, TC), BF),
        in_specs=[vmem] * 12,
        out_specs=vmem,
        scratch_shapes=[
            pltpu.VMEM((24, 2, 64, 256), BF),
            pltpu.VMEM((96, 64, 256), BF),
            pltpu.VMEM((96, 192, 128), F32),
            pltpu.VMEM((3, 64, 256), F32),
            pltpu.VMEM((2, 64, 128), F32),
            pltpu.VMEM((64, 128), F32),
        ],
        compiler_params=pltpu.CompilerParams(vmem_limit_bytes=VMEM_BYTES),
    )(got, outer, top, top_outer, bottom, bottom_outer, gathered, first_refine, second_refine, biases,
      jnp.asarray(main_table, BF), jnp.asarray(rim_table, BF))


def per_device(coarse_feats, fine_feats, pair_prior, zoom_start, coarse_weights, coarse_bias,
               refine_first, refine_second, refine_bias):
    *held, gathered = gather(coarse_feats, fine_feats, pair_prior)
    gathered = gathered.reshape(SIDE, 128)
    coarse_map, *moved = lax.cond(
        zoom_start[0] == 0,
        functools.partial(coarse, 0),
        functools.partial(coarse, 1),
        *held, gathered, coarse_weights, refine_first, coarse_bias,
    )
    refined = refine(mesh_place, *moved, gathered, refine_first, refine_second, refine_bias)
    return coarse_map, refined


def solution(mesh):
    return jax.shard_map(
        per_device,
        mesh=mesh,
        in_specs=(
            P(None, ("row", "col")),
            P(None, ("row", "col")),
            P(None, "row", "col"),
            P(),
            P(),
            P(),
            P(),
            P(),
            P(),
        ),
        out_specs=(P(None, "row", "col"), P(None, "row", "col")),
        check_vma=False,
    )
```

```python
import functools

import jax
import jax.numpy as jnp
import numpy as np
from jax import lax
from jax.experimental import pallas as pl
from jax.experimental.pallas import tpu as pltpu
from jax.sharding import PartitionSpec as P

BF = jnp.bfloat16
F32 = jnp.float32
MESH = pl.DeviceIdType.MESH
VMEM_BYTES = 48 << 20
SIDE = 1024
ROWS, COLS = 16, 8
TR, TC = 64, 128

vmem = pl.BlockSpec(memory_space=pltpu.VMEM)
anywhere = pl.BlockSpec(memory_space=pl.ANY)


def lanes_of(shape):
    return lax.broadcasted_iota(jnp.int32, shape, len(shape) - 1)


def column_offsets(shape):
    lane = lanes_of(shape)
    return jnp.where(lane < 192, lane, lane - 256)


def shifted_stack(x, spacing, width):
    return jnp.concatenate(
        [
            pltpu.roll(x, spacing, 1)[:, :width],
            x[:, :width],
            pltpu.roll(x, 256 - spacing, 1)[:, :width],
        ],
        axis=0,
    )


def tap_products(w, source, first, target, into, count, group, spacing, width):
    for g in range(count // group):
        base = first + g * group
        stack = jnp.concatenate(
            [shifted_stack(source[base + t], spacing, width) for t in range(group)], axis=1
        )
        product = jnp.dot(w, stack, preferred_element_type=F32)
        for t in range(group):
            target[into + g * group + t] = product[:, t * width : (t + 1) * width]


def carry_taps(target, spacing):
    last = target.shape[0] - 2 * spacing
    for t in range(2 * spacing):
        target[t, 0:64] = target[last + t, 0:64]
        if t >= spacing:
            target[t, 64:128] = target[last + t, 64:128]


def tap_sum(target, i, spacing, width):
    return (
        target[i, 0:64, 0:width]
        + target[i + spacing, 64:128, 0:width]
        + target[i + 2 * spacing, 128:192, 0:width]
    )


def bias_columns(bias, layer, width):
    row = jnp.broadcast_to(bias[layer : layer + 1, :], (128, 64))
    column = jnp.transpose(row)
    return column if width == 128 else jnp.concatenate([column, column], axis=1)


def halves_joined(a, b, c, upper):
    low = lanes_of(a.shape) < 64
    if upper:
        first = jnp.where(low, pltpu.roll(a, 64, 1), b)
        return jnp.concatenate([first, pltpu.roll(c, 64, 1)[:, :64]], axis=1)
    first = jnp.where(low, a, pltpu.roll(b, 64, 1))
    return jnp.concatenate([first, c[:, :64]], axis=1)


def gather_kernel(coarse_feats, fine_feats, prior, tile, rows, rim_left, rim_right, gathered,
                  feats, left, right, send, recv, send_a, recv_a, send_b, recv_b, own):
    r, c = lax.axis_index("row"), lax.axis_index("col")
    up, down = lax.rem(r + ROWS - 1, ROWS), lax.rem(r + 1, ROWS)
    west, east = lax.rem(c + COLS - 1, COLS), lax.rem(c + 1, COLS)
    has_up, has_down, has_west, has_east = r > 0, r < ROWS - 1, c > 0, c < COLS - 1
    barrier = pltpu.get_barrier_semaphore()

    def greet(to):
        pl.semaphore_signal(barrier, 1, device_id=to, device_id_type=MESH)

    for d in range(1, COLS):
        greet((r, lax.rem(c + d, COLS)))
    for d in range(1, ROWS):
        greet((lax.rem(r + d, ROWS), c))
    peers = COLS - 1 + ROWS - 1
    for a, has_a in ((up, has_up), (down, has_down)):
        for b, has_b in ((west, has_west), (east, has_east)):
            pl.when(has_a & has_b)(functools.partial(greet, (a, b)))
            peers = peers + jnp.where(has_a & has_b, 1, 0)

    both = jnp.concatenate([coarse_feats[...], fine_feats[...]], axis=0).astype(F32)
    feats[...] = jnp.transpose(both).astype(BF)
    for q in range(4):
        tile[16 * q : 16 * q + 16] = jnp.swapaxes(prior[:, 16 * q : 16 * q + 16, :], 0, 1)
    part = lanes_of((64, 128)) // 16

    def pack(q, carry):
        low = tile[8 * q]
        high = pltpu.roll(low, 16, 1)
        for k in range(1, 8):
            x = tile[8 * q + k]
            low = jnp.where(part == k, pltpu.roll(x, 16 * k, 1), low)
            high = jnp.where(part == k, pltpu.roll(x, (16 * k + 16) % 128, 1), high)
        left[q] = low
        right[q] = high
        return carry

    def copy(source, target, out_sem, in_sem, to):
        return pltpu.make_async_remote_copy(
            src_ref=source,
            dst_ref=target,
            send_sem=out_sem,
            recv_sem=in_sem,
            device_id=to,
            device_id_type=MESH,
        )

    pl.semaphore_wait(barrier, peers)
    place = r * COLS + c
    mine = pltpu.make_async_copy(feats, gathered.at[place], own)
    mine.start()
    first = [
        copy(feats, gathered.at[place], send_a.at[d], recv_a.at[d], (r, lax.rem(c + d, COLS)))
        for d in range(1, COLS)
    ]
    for x in first:
        x.start()
    lax.fori_loop(0, 8, pack, 0)
    rims = [
        (right, rim_left.at[pl.ds(2, 8)], (r, east), has_east, has_west),
        (left, rim_right.at[pl.ds(2, 8)], (r, west), has_west, has_east),
        (tile.at[pl.ds(54, 10)], rows.at[0], (down, c), has_down, has_up),
        (tile.at[pl.ds(0, 10)], rows.at[1], (up, c), has_up, has_down),
        (right.at[pl.ds(6, 2)], rim_left.at[pl.ds(0, 2)], (down, east),
         has_down & has_east, has_up & has_west),
        (right.at[pl.ds(0, 2)], rim_left.at[pl.ds(10, 2)], (up, east),
         has_up & has_east, has_down & has_west),
        (left.at[pl.ds(6, 2)], rim_right.at[pl.ds(0, 2)], (down, west),
         has_down & has_west, has_up & has_east),
        (left.at[pl.ds(0, 2)], rim_right.at[pl.ds(10, 2)], (up, west),
         has_up & has_west, has_down & has_east),
    ]
    rims = [
        (copy(s, t, send.at[k], recv.at[k], to), out, into)
        for k, (s, t, to, out, into) in enumerate(rims)
    ]
    for x, out, _ in rims:
        pl.when(out)(x.start)
    mine.wait()
    for x in first:
        x.wait_recv()
    block = gathered.at[pl.ds(r * COLS, COLS)]
    second = [
        copy(block, block, send_b.at[d], recv_b.at[d], (lax.rem(r + d, ROWS), c))
        for d in range(1, ROWS)
    ]
    for x in second:
        x.start()
    for x in first:
        x.wait_send()
    for x, out, into in rims:
        pl.when(out)(x.wait_send)
        pl.when(into)(x.wait_recv)
    for x in second:
        x.wait()


def gather(coarse_feats, fine_feats, prior):
    return pl.pallas_call(
        gather_kernel,
        out_shape=(
            jax.ShapeDtypeStruct((TR, 64, TC), BF),
            jax.ShapeDtypeStruct((2, 10, 64, TC), BF),
            jax.ShapeDtypeStruct((12, 64, TC), BF),
            jax.ShapeDtypeStruct((12, 64, TC), BF),
            jax.ShapeDtypeStruct((ROWS * COLS, 8, TC), BF),
        ),
        in_specs=[vmem] * 3,
        out_specs=(vmem,) + (anywhere,) * 4,
        scratch_shapes=[
            pltpu.VMEM((8, TC), BF),
            pltpu.VMEM((8, 64, TC), BF),
            pltpu.VMEM((8, 64, TC), BF),
            pltpu.SemaphoreType.DMA((8,)),
            pltpu.SemaphoreType.DMA((8,)),
            pltpu.SemaphoreType.DMA((COLS,)),
            pltpu.SemaphoreType.DMA((COLS,)),
            pltpu.SemaphoreType.DMA((ROWS,)),
            pltpu.SemaphoreType.DMA((ROWS,)),
            pltpu.SemaphoreType.DMA,
        ],
        compiler_params=pltpu.CompilerParams(
            collective_id=1, has_side_effects=True, vmem_limit_bytes=VMEM_BYTES
        ),
    )(coarse_feats, fine_feats, prior)


def chosen_bins(gathered, first, ring):
    lanes = 256 if ring else 128
    shape = (SIDE, lanes)
    wanted = first + (column_offsets(shape) if ring else lanes_of(shape))
    picked = lax.broadcasted_iota(jnp.int32, shape, 0) == wanted
    return lax.dot_general(
        gathered[...],
        jnp.where(picked, 1.0, 0.0).astype(BF),
        (((0,), (0,)), ((), ())),
        preferred_element_type=F32,
    )


def spread_tables():
    lane = np.arange(128)
    source = np.arange(128)[:, None]
    main = np.stack([source == 64 * k + lane[None] // 2 for k in range(2)])
    rim = np.zeros((256, 16, 128), bool)
    for k in range(16):
        rim[:128, k] = (source == 8 * k + lane[None] // 2) & (lane[None] < 16)
        rim[128:, k] = (source == 8 * k + (lane[None] - 112) // 2) & (lane[None] >= 112)
    return main.astype(np.float32), rim.reshape(256, 2048).astype(np.float32)


def decoder_kernel(half, tile, rows, rim_left, rim_right, gathered, weights, first_refine,
                   second_refine, coarse_bias, refine_bias, main_table, rim_table,
                   map_out, refined,
                   x, taps1, hidden, taps2, fields, taps3, w3, bias, fr, fc, pieces,
                   got, sides, top, bottom, side_in, wide, fine, taps4, row_terms, row_part,
                   send, recv, own, send_n, recv_n):
    r, c = lax.axis_index("row"), lax.axis_index("col")
    base_r, base_c = half * (ROWS // 2), half * (COLS // 2)
    up, down = lax.rem(r + ROWS - 1, ROWS), lax.rem(r + 1, ROWS)
    west, east = lax.rem(c + COLS - 1, COLS), lax.rem(c + 1, COLS)
    has_up, has_down, has_west, has_east = r > 0, r < ROWS - 1, c > 0, c < COLS - 1
    from_r, from_c = base_r + r // 2, base_c + c // 2
    remote_main = (from_r != r) | (from_c != c)
    is_source = (r >= base_r) & (r < base_r + ROWS // 2) & (c >= base_c) & (c < base_c + COLS // 2)
    local_r, local_c = r - base_r, c - base_c

    def main_to(t, h):
        return 2 * local_r + t, 2 * local_c + h

    def away(to):
        return (to[0] != r) | (to[1] != c)

    barrier = pltpu.get_barrier_semaphore()

    def greet(to):
        pl.semaphore_signal(barrier, 1, device_id=to, device_id_type=MESH)

    around = [
        ((up, c), has_up),
        ((down, c), has_down),
        ((r, west), has_west),
        ((r, east), has_east),
        ((up, west), has_up & has_west),
        ((up, east), has_up & has_east),
        ((down, west), has_down & has_west),
        ((down, east), has_down & has_east),
    ]
    met = around + [((from_r, from_c), remote_main)]
    met += [(main_to(t, k), is_source & away(main_to(t, k))) for t in range(2) for k in range(2)]
    peers = 0
    for to, there in met:
        pl.when(there)(functools.partial(greet, to))
        peers = peers + jnp.where(there, 1, 0)

    def copy(source, target, out_sem, in_sem, to):
        return pltpu.make_async_remote_copy(
            src_ref=source,
            dst_ref=target,
            send_sem=out_sem,
            recv_sem=in_sem,
            device_id=to,
            device_id_type=MESH,
        )

    def piece(j, k):
        t, q = j // 2, lax.rem(j, 2)
        return copy(pieces.at[k, t, pl.ds(8 * q, 8)], got.at[pl.ds(8 * q, 8)],
                    send.at[2 * j + k], recv.at[q], main_to(t, k))

    def stay(j, k):
        t, q = j // 2, lax.rem(j, 2)
        return pltpu.make_async_copy(
            pieces.at[k, t, pl.ds(8 * q, 8)], got.at[pl.ds(8 * q, 8)], own.at[q]
        )

    w1 = weights[0].reshape(192, 192)
    w2 = weights[1].reshape(192, 192)
    joined = first_refine[...].reshape(192, 384)
    w3[...] = halves_joined(joined[:, 0:128], joined[:, 128:256], joined[:, 256:384], False)
    bias[0] = bias_columns(coarse_bias, 0, 256)
    bias[1] = bias_columns(coarse_bias, 1, 256)
    row0, col0 = r * TR, c * TC
    fr[...] = chosen_bins(gathered, row0 - 16, False)[0:64]
    fc[...] = chosen_bins(gathered, col0, True)[0:64]
    cols = col0 + column_offsets((64, 256))
    in_cols = (cols >= 0) & (cols < SIDE)
    half_c, half_r = lax.rem(c, COLS // 2) * TC, lax.rem(r, ROWS // 2) * TR
    cols_q = half_c + column_offsets((64, 256))
    in_quarter = (cols_q >= 0) & (cols_q < SIDE // 2)
    low_half = lanes_of((64, 128)) < 64

    def pair_row(q, k, at, body, shift):
        rim = jnp.where(
            low_half,
            pltpu.roll(rim_right[q], (128 - 16 * k) % 128, 1),
            pltpu.roll(rim_left[q], 112 - 16 * k, 1),
        )
        prior = jnp.concatenate([body, rim], axis=1).astype(F32)
        value = prior + (fc[...] + shift[:, k : k + 1])
        grow = row0 + 8 * q + k - 16
        inside = in_cols & (grow >= 0) & (grow < SIDE)
        x[at] = jnp.where(inside, value, 0.0).astype(BF)

    def features_at(q):
        return pltpu.roll(fr[...], lax.rem(256 - 8 * q, 128), 1)

    def rim_rows(side):
        for k in range(10):
            row = 64 + k if side else k - 10
            q = (row + 16) // 8
            pair_row(q, row % 8, row + 10, rows[side, k], features_at(q))

    def own_rows(g):
        shift = features_at(g + 2)
        for k in range(8):
            pair_row(g + 2, k, 8 * g + k + 10, tile[8 * g + k], shift)

    def hidden_rows(first, taken, count):
        for t in range(count):
            at = first + t
            grow = row0 + at - 8
            value = jnp.maximum(tap_sum(taps1, taken + t, 2, 256) + bias[0], 0.0)
            inside = in_cols & (grow >= 0) & (grow < SIDE)
            hidden[at] = jnp.where(inside, value, 0.0).astype(BF)

    def field_rows(first, taken, count):
        for t in range(count):
            at = first + t
            qrow = half_r + at - 4
            value = jnp.maximum(tap_sum(taps2, taken + t, 4, 256) + bias[1], 0.0)
            inside = in_quarter & (qrow >= 0) & (qrow < SIDE // 2)
            fields[at] = jnp.where(inside, value, 0.0).astype(BF)

    def pack(j):
        t, q = j // 2, lax.rem(j, 2)
        for k in range(0, 16, 2):
            v = tap_sum(taps3, k, 4, 128).astype(BF)
            u = tap_sum(taps3, k + 1, 4, 128).astype(BF)
            at = 8 * q + k // 2
            pieces[0, t, at] = jnp.where(low_half, v, pltpu.roll(u, 64, 1))
            pieces[1, t, at] = jnp.where(low_half, pltpu.roll(v, 64, 1), u)

    rim_rows(0)

    def early_rows(g, carry):
        own_rows(g)
        return carry

    lax.fori_loop(0, 4, early_rows, 0)
    tap_products(w1, x, 0, taps1, 0, 20, 10, 2, 256)
    hidden_rows(0, 0, 16)
    tap_products(w2, hidden, 0, taps2, 8, 16, 8, 4, 256)
    field_rows(0, 8, 8)
    tap_products(w3[...], fields, 0, taps3, 16, 8, 8, 4, 128)
    pl.semaphore_wait(barrier, peers)

    def chunk(j, carry):
        @pl.when((j == 1) | (j == 2))
        def _():
            own_rows(2 * j + 2)
            own_rows(2 * j + 3)

        pl.when(j == 3)(lambda: rim_rows(1))
        carry_taps(taps1, 2)
        carry_taps(taps2, 4)
        carry_taps(taps3, 4)
        tap_products(w1, x, 20 + 16 * j, taps1, 4, 16, 8, 2, 256)
        hidden_rows(16 + 16 * j, 0, 16)
        tap_products(w2, hidden, 16 + 16 * j, taps2, 8, 16, 8, 4, 256)
        field_rows(8 + 16 * j, 0, 16)
        tap_products(w3[...], fields, 8 + 16 * j, taps3, 8, 16, 8, 4, 128)
        pack(j)
        for k in range(2):
            pl.when(is_source & away(main_to(j // 2, k)))(lambda k=k: piece(j, k).start())
            pl.when(is_source & jnp.logical_not(away(main_to(j // 2, k))))(
                lambda k=k: stay(j, k).start()
            )
        return carry

    lax.fori_loop(0, 4, chunk, 0)
    for q in range(4):
        map_out[:, 16 * q : 16 * q + 16, :] = jnp.swapaxes(
            fields[4 + 16 * q : 20 + 16 * q, :, 0:128], 0, 1
        )

    wq = halves_joined(joined[:, 0:128], joined[:, 128:256], joined[:, 256:384], True)
    wp = jnp.concatenate(
        [
            halves_joined(*[first_refine[a, :, 128 * e : 128 * e + 128] for a in range(3)], True)
            for e in range(3)
        ],
        axis=0,
    )
    w4 = second_refine[...].reshape(192, 192)
    fine_c = chosen_bins(gathered, col0, True)[64:128].astype(BF)
    terms = jnp.dot(wq, shifted_stack(fine_c, 8, 256), preferred_element_type=F32)
    base = terms[64:128] + bias_columns(refine_bias, 0, 256)
    row_terms[0] = base + terms[0:64] + terms[128:192]
    row_terms[1] = base + terms[128:192]
    row_terms[2] = base + terms[0:64]
    fine_r = chosen_bins(gathered, row0 - 24, False)[64:128].astype(BF)
    stack = jnp.concatenate([pltpu.roll(fine_r, 8, 1), fine_r, pltpu.roll(fine_r, 120, 1)], axis=0)
    terms = jnp.dot(wp, stack, preferred_element_type=F32)
    row_part[0] = terms[0:64] + terms[64:128] + terms[128:192]
    row_part[1] = terms[64:128] + jnp.where(c == 0, terms[128:192], terms[0:64])
    bias[0] = bias_columns(refine_bias, 1, 256)

    def spread_main(source, first, count, at):
        for k in range(2):
            value = jnp.dot(
                source[first : first + count].reshape(count * 64, 128),
                main_table[k],
                preferred_element_type=F32,
            )
            wide[at : at + count, k, :, 0:128] = value.reshape(count, 64, 128).astype(BF)

    part = lanes_of((64, 128)) // 8
    for q in range(2):
        pl.when(remote_main)(lambda: piece(q, 0).wait_recv())
        pl.when(jnp.logical_not(remote_main))(lambda: stay(q, 0).wait())
        low = high = None
        for k in range(16):
            v = got[8 * q + k // 2]
            first = (8 * k - 64 * (k % 2)) % 128
            moved, other = pltpu.roll(v, first, 1), pltpu.roll(v, (first - 56) % 128, 1)
            low = moved if k == 0 else jnp.where(part == k, moved, low)
            high = other if k == 0 else jnp.where(part == k, other, high)
        sides[0, q] = low
        sides[1, q] = high
    rims = [
        (got.at[pl.ds(12, 4)], top, (down, c), has_down, has_up),
        (got.at[pl.ds(0, 4)], bottom, (up, c), has_up, has_down),
        (sides.at[0], side_in.at[1, pl.ds(1, 2)], (r, west), has_west, has_east),
        (sides.at[1], side_in.at[0, pl.ds(1, 2)], (r, east), has_east, has_west),
        (sides.at[0, 1], side_in.at[1, 0], (down, west),
         has_down & has_west, has_up & has_east),
        (sides.at[1, 1], side_in.at[0, 0], (down, east),
         has_down & has_east, has_up & has_west),
        (sides.at[0, 0], side_in.at[1, 3], (up, west),
         has_up & has_west, has_down & has_east),
        (sides.at[1, 0], side_in.at[0, 3], (up, east),
         has_up & has_east, has_down & has_west),
    ]
    rims = [
        (copy(s, t, send_n.at[k], recv_n.at[k], to), out, into)
        for k, (s, t, to, out, into) in enumerate(rims)
    ]
    for y, out, _ in rims:
        pl.when(out)(y.start)

    offsets = column_offsets((64, 256)) + col0
    inside_of = [(offsets >= 0) & (offsets < SIDE)]
    edge_of = [(offsets < 8) | (offsets >= SIDE - 8)]

    def fine_rows(g, at):
        lanes = slice(at, at + 128)
        grow0 = row0 + 8 * g - 16
        inside = inside_of[0][:, lanes] & (grow0 >= 0) & (grow0 < SIDE)
        variant = jnp.where(grow0 == 0, 1, jnp.where(grow0 == SIDE - 8, 2, 0))
        shift = lax.rem(256 - 8 * g - 8, 128)
        everywhere = pltpu.roll(row_part[0], shift, 1)
        edge = pltpu.roll(row_part[1], shift, 1)
        column_terms = row_terms[variant, :, lanes]
        for k in range(8):
            row = jnp.where(edge_of[0][:, lanes], edge[:, k : k + 1], everywhere[:, k : k + 1])
            value = wide[2 * g + k // 4, (k // 2) % 2, :, lanes].astype(F32) + (column_terms + row)
            fine[8 * g + k, :, lanes] = jnp.where(inside, jnp.maximum(value, 0.0), 0.0).astype(BF)

    def own_fine_rows(g, carry):
        fine_rows(g, 0)
        return carry

    def side_fine_rows(g, carry):
        fine_rows(g, 128)
        return carry

    spread_main(got, 0, 16, 4)
    lax.fori_loop(2, 10, own_fine_rows, 0)
    for j in range(4):
        for k in range(2):
            pl.when(is_source & away(main_to(j // 2, k)))(lambda: piece(j, k).wait_send())
    for y, out, into in rims:
        pl.when(out)(y.wait_send)
        pl.when(into)(y.wait_recv)
    spread_main(top, 0, 4, 0)
    spread_main(bottom, 0, 4, 20)

    def spread_rim(tile_at, low, high, first):
        both = jnp.concatenate(
            [
                jnp.where(has_east, side_in[1, tile_at].astype(F32), 0.0),
                jnp.where(has_west, side_in[0, tile_at].astype(F32), 0.0),
            ],
            axis=1,
        ).astype(BF)
        value = jnp.dot(
            both, rim_table[:, 128 * low : 128 * high], preferred_element_type=F32
        ).astype(BF)
        for k in range(high - low):
            row = first + k
            wide[row // 2, row % 2, :, 128:256] = value[:, 128 * k : 128 * k + 128]

    spread_rim(0, 8, 16, 0)
    spread_rim(1, 0, 16, 8)
    spread_rim(2, 0, 16, 24)
    spread_rim(3, 0, 8, 40)
    for g in (0, 1, 10, 11):
        fine_rows(g, 0)
    lax.fori_loop(0, 12, side_fine_rows, 0)

    def last_products(g, carry):
        tap_products(w4, fine, 16 * g, taps4, 16 * g, 16, 8, 16, 128)
        return carry

    lax.fori_loop(0, 6, last_products, 0)
    for g in range(4):
        value = jnp.stack(
            [
                jnp.maximum(tap_sum(taps4, 16 * g + k, 16, 128) + bias[0, :, 0:128], 0.0).astype(BF)
                for k in range(16)
            ]
        )
        refined[:, 16 * g : 16 * g + 16, :] = jnp.swapaxes(value, 0, 1)


def decoder(half, tile, rows, rim_left, rim_right, gathered, weights, first_refine,
            second_refine, coarse_bias, refine_bias, main_table, rim_table):
    return pl.pallas_call(
        functools.partial(decoder_kernel, half),
        out_shape=(
            jax.ShapeDtypeStruct((64, TR, TC), BF),
            jax.ShapeDtypeStruct((64, TR, TC), BF),
        ),
        in_specs=[vmem] * 12,
        out_specs=(vmem, vmem),
        scratch_shapes=[
            pltpu.VMEM((84, 64, 256), BF),
            pltpu.VMEM((20, 192, 256), F32),
            pltpu.VMEM((80, 64, 256), BF),
            pltpu.VMEM((24, 192, 256), F32),
            pltpu.VMEM((72, 64, 256), BF),
            pltpu.VMEM((24, 192, 128), F32),
            pltpu.VMEM((192, 192), BF),
            pltpu.VMEM((2, 64, 256), F32),
            pltpu.VMEM((64, 128), F32),
            pltpu.VMEM((64, 256), F32),
            pltpu.VMEM((2, 2, 16, 64, 128), BF),
            pltpu.VMEM((16, 64, 128), BF),
            pltpu.VMEM((2, 2, 64, 128), BF),
            pltpu.VMEM((4, 64, 128), BF),
            pltpu.VMEM((4, 64, 128), BF),
            pltpu.VMEM((2, 4, 64, 128), BF),
            pltpu.VMEM((24, 2, 64, 256), BF),
            pltpu.VMEM((96, 64, 256), BF),
            pltpu.VMEM((96, 192, 128), F32),
            pltpu.VMEM((3, 64, 256), F32),
            pltpu.VMEM((2, 64, 128), F32),
            pltpu.SemaphoreType.DMA((8,)),
            pltpu.SemaphoreType.DMA((2,)),
            pltpu.SemaphoreType.DMA((2,)),
            pltpu.SemaphoreType.DMA((8,)),
            pltpu.SemaphoreType.DMA((8,)),
        ],
        compiler_params=pltpu.CompilerParams(
            collective_id=2 + half, has_side_effects=True, vmem_limit_bytes=VMEM_BYTES
        ),
    )(tile, rows, rim_left, rim_right, gathered, weights, first_refine,
      second_refine, coarse_bias, refine_bias, main_table, rim_table)


def per_device(coarse_feats, fine_feats, pair_prior, zoom_start, coarse_weights, coarse_bias,
               refine_first, refine_second, refine_bias):
    *held, gathered = gather(coarse_feats, fine_feats, pair_prior)
    gathered = gathered.reshape(SIDE, 128)
    main_table, rim_table = spread_tables()
    return lax.cond(
        zoom_start[0] == 0,
        functools.partial(decoder, 0),
        functools.partial(decoder, 1),
        *held, gathered, coarse_weights, refine_first, refine_second, coarse_bias, refine_bias,
        jnp.asarray(main_table, BF), jnp.asarray(rim_table, BF),
    )


def solution(mesh):
    return jax.shard_map(
        per_device,
        mesh=mesh,
        in_specs=(
            P(None, ("row", "col")),
            P(None, ("row", "col")),
            P(None, "row", "col"),
            P(),
            P(),
            P(),
            P(),
            P(),
            P(),
        ),
        out_specs=(P(None, "row", "col"), P(None, "row", "col")),
        check_vma=False,
    )
```

```python
import functools

import jax
import jax.numpy as jnp
import numpy as np
from jax import lax
from jax.experimental import pallas as pl
from jax.experimental.pallas import tpu as pltpu
from jax.sharding import PartitionSpec as P

BF = jnp.bfloat16
F32 = jnp.float32
MESH = pl.DeviceIdType.MESH
VMEM_BYTES = 58 << 20
SIDE = 1024
ROWS, COLS = 16, 8
TR, TC = 64, 128

anywhere = pl.BlockSpec(memory_space=pl.ANY)


def lanes_of(shape):
    return lax.broadcasted_iota(jnp.int32, shape, len(shape) - 1)


def column_offsets(shape):
    lane = lanes_of(shape)
    return jnp.where(lane < 192, lane, lane - 256)


def shifted_stack(x, spacing, width):
    return jnp.concatenate(
        [
            pltpu.roll(x, spacing, 1)[:, :width],
            x[:, :width],
            pltpu.roll(x, 256 - spacing, 1)[:, :width],
        ],
        axis=0,
    )


def tap_products(w, source, first, target, into, count, group, spacing, width):
    for g in range(count // group):
        base = first + g * group
        stack = jnp.concatenate(
            [shifted_stack(source[base + t], spacing, width) for t in range(group)], axis=1
        )
        product = jnp.dot(w, stack, preferred_element_type=F32)
        for t in range(group):
            target[into + g * group + t] = product[:, t * width : (t + 1) * width]


def carry_taps(target, spacing):
    last = target.shape[0] - 2 * spacing
    for t in range(2 * spacing):
        target[t, 0:64] = target[last + t, 0:64]
        if t >= spacing:
            target[t, 64:128] = target[last + t, 64:128]


def tap_sum(target, i, spacing, width):
    return (
        target[i, 0:64, 0:width]
        + target[i + spacing, 64:128, 0:width]
        + target[i + 2 * spacing, 128:192, 0:width]
    )


def bias_columns(bias, layer, width):
    row = jnp.broadcast_to(bias[layer : layer + 1, :], (128, 64))
    column = jnp.transpose(row)
    return column if width == 128 else jnp.concatenate([column, column], axis=1)


def halves_joined(a, b, c, upper):
    low = lanes_of(a.shape) < 64
    if upper:
        first = jnp.where(low, pltpu.roll(a, 64, 1), b)
        return jnp.concatenate([first, pltpu.roll(c, 64, 1)[:, :64]], axis=1)
    first = jnp.where(low, a, pltpu.roll(b, 64, 1))
    return jnp.concatenate([first, c[:, :64]], axis=1)


def chosen_bins(gathered, first, ring):
    lanes = 256 if ring else 128
    shape = (SIDE, lanes)
    wanted = first + (column_offsets(shape) if ring else lanes_of(shape))
    picked = lax.broadcasted_iota(jnp.int32, shape, 0) == wanted
    return lax.dot_general(
        gathered,
        jnp.where(picked, 1.0, 0.0).astype(BF),
        (((0,), (0,)), ((), ())),
        preferred_element_type=F32,
    )


def spread_tables():
    lane = np.arange(128)
    source = np.arange(128)[:, None]
    main = np.stack([source == 64 * k + lane[None] // 2 for k in range(2)])
    rim = np.zeros((256, 16, 128), bool)
    for k in range(16):
        rim[:128, k] = (source == 8 * k + lane[None] // 2) & (lane[None] < 16)
        rim[128:, k] = (source == 8 * k + (lane[None] - 112) // 2) & (lane[None] >= 112)
    return main.astype(np.float32), rim.reshape(256, 2048).astype(np.float32)


def decoder_kernel(half, coarse_feats, fine_feats, prior, coarse_weights, first_weights,
                   second_weights, coarse_biases, refine_biases, tables_main, tables_rim,
                   map_result, refined_result,
                   whole, weights, first_refine, second_refine, coarse_bias, refine_bias,
                   main_table, rim_table,
                   tile, rows, rim_left, rim_right, left, right, feats, gathered, map_out, refined,
                   x, taps1, hidden, taps2, fields, taps3, w3, bias, fr, fc, fine_r, fine_c, pieces,
                   got, sides, top, bottom, side_in, wide, fine, taps4, row_terms, row_part,
                   send, recv, own, send_n, recv_n,
                   load, send_f, recv_f, send_a, recv_a, send_b, recv_b):
    loads = [
        (prior, whole),
        (coarse_feats, feats.at[0]),
        (fine_feats, feats.at[1]),
        (coarse_weights, weights),
        (first_weights, first_refine),
        (second_weights, second_refine),
        (coarse_biases, coarse_bias),
        (refine_biases, refine_bias),
        (tables_main, main_table),
        (tables_rim, rim_table),
    ]
    loads = [pltpu.make_async_copy(s, d, load.at[k]) for k, (s, d) in enumerate(loads)]
    for y in loads:
        y.start()
    r, c = lax.axis_index("row"), lax.axis_index("col")
    base_r, base_c = half * (ROWS // 2), half * (COLS // 2)
    up, down = lax.rem(r + ROWS - 1, ROWS), lax.rem(r + 1, ROWS)
    west, east = lax.rem(c + COLS - 1, COLS), lax.rem(c + 1, COLS)
    has_up, has_down, has_west, has_east = r > 0, r < ROWS - 1, c > 0, c < COLS - 1
    from_r, from_c = base_r + r // 2, base_c + c // 2
    remote_main = (from_r != r) | (from_c != c)
    is_source = (r >= base_r) & (r < base_r + ROWS // 2) & (c >= base_c) & (c < base_c + COLS // 2)
    local_r, local_c = r - base_r, c - base_c

    def main_to(t, h):
        return 2 * local_r + t, 2 * local_c + h

    def away(to):
        return (to[0] != r) | (to[1] != c)

    barrier = pltpu.get_barrier_semaphore()

    def greet(to):
        pl.semaphore_signal(barrier, 1, device_id=to, device_id_type=MESH)

    around = [
        ((up, c), has_up),
        ((down, c), has_down),
        ((r, west), has_west),
        ((r, east), has_east),
        ((up, west), has_up & has_west),
        ((up, east), has_up & has_east),
        ((down, west), has_down & has_west),
        ((down, east), has_down & has_east),
    ]
    met = around[4:] + [((from_r, from_c), remote_main)]
    met += [(main_to(t, k), is_source & away(main_to(t, k))) for t in range(2) for k in range(2)]
    for d in range(1, COLS):
        greet((r, lax.rem(c + d, COLS)))
    for d in range(1, ROWS):
        greet((lax.rem(r + d, ROWS), c))
    peers = COLS - 1 + ROWS - 1
    for to, there in met:
        pl.when(there)(functools.partial(greet, to))
        peers = peers + jnp.where(there, 1, 0)

    def copy(source, target, out_sem, in_sem, to):
        return pltpu.make_async_remote_copy(
            src_ref=source,
            dst_ref=target,
            send_sem=out_sem,
            recv_sem=in_sem,
            device_id=to,
            device_id_type=MESH,
        )

    def piece(j, k):
        t, q = j // 2, lax.rem(j, 2)
        return copy(pieces.at[k, t, pl.ds(8 * q, 8)], got.at[pl.ds(8 * q, 8)],
                    send.at[2 * j + k], recv.at[q], main_to(t, k))

    def stay(j, k):
        t, q = j // 2, lax.rem(j, 2)
        return pltpu.make_async_copy(
            pieces.at[k, t, pl.ds(8 * q, 8)], got.at[pl.ds(8 * q, 8)], own.at[q]
        )

    for y in loads[1:]:
        y.wait()
    joined = first_refine[...].reshape(192, 384)
    w3[...] = halves_joined(joined[:, 0:128], joined[:, 128:256], joined[:, 256:384], False)
    bias[0] = bias_columns(coarse_bias, 0, 256)
    bias[1] = bias_columns(coarse_bias, 1, 256)
    place = r * COLS + c
    gathered[place] = jnp.concatenate([feats[0], feats[1]], axis=1)
    loads[0].wait()
    for q in range(4):
        tile[16 * q : 16 * q + 16] = jnp.swapaxes(whole[:, 16 * q : 16 * q + 16, :], 0, 1)
    pl.semaphore_wait(barrier, peers)
    first = [
        copy(gathered.at[place], gathered.at[place], send_a.at[d], recv_a.at[d],
             (r, lax.rem(c + d, COLS)))
        for d in range(1, COLS)
    ]
    for y in first:
        y.start()
    sixteenth = lanes_of((64, 128)) // 16

    def pack_edges(q, carry):
        low = tile[8 * q]
        high = pltpu.roll(low, 16, 1)
        for k in range(1, 8):
            v = tile[8 * q + k]
            low = jnp.where(sixteenth == k, pltpu.roll(v, 16 * k, 1), low)
            high = jnp.where(sixteenth == k, pltpu.roll(v, (16 * k + 16) % 128, 1), high)
        left[q] = low
        right[q] = high
        return carry

    lax.fori_loop(0, 8, pack_edges, 0)
    outlines = [
        (right, rim_left.at[pl.ds(2, 8)], (r, east), has_east, has_west),
        (left, rim_right.at[pl.ds(2, 8)], (r, west), has_west, has_east),
        (tile.at[pl.ds(54, 10)], rows.at[0], (down, c), has_down, has_up),
        (tile.at[pl.ds(0, 10)], rows.at[1], (up, c), has_up, has_down),
        (right.at[pl.ds(6, 2)], rim_left.at[pl.ds(0, 2)], (down, east),
         has_down & has_east, has_up & has_west),
        (right.at[pl.ds(0, 2)], rim_left.at[pl.ds(10, 2)], (up, east),
         has_up & has_east, has_down & has_west),
        (left.at[pl.ds(6, 2)], rim_right.at[pl.ds(0, 2)], (down, west),
         has_down & has_west, has_up & has_east),
        (left.at[pl.ds(0, 2)], rim_right.at[pl.ds(10, 2)], (up, west),
         has_up & has_west, has_down & has_east),
    ]
    outlines = [
        (copy(s, t, send_f.at[k], recv_f.at[k], to), out, into)
        for k, (s, t, to, out, into) in enumerate(outlines)
    ]
    for y, out, _ in outlines:
        pl.when(out)(y.start)
    for y in first:
        y.wait_recv()
    block = gathered.at[pl.ds(r * COLS, COLS)]
    second = [
        copy(block, block, send_b.at[d], recv_b.at[d], (lax.rem(r + d, ROWS), c))
        for d in range(1, ROWS)
    ]
    for y in second:
        y.start()
    for y in second:
        y.wait_recv()

    row0, col0 = r * TR, c * TC
    every_bin = gathered[...].reshape(SIDE, 128)
    picked = chosen_bins(every_bin, row0 - 24, False)
    fr[...] = picked[0:64]
    fine_r[...] = picked[64:128].astype(BF)
    picked = chosen_bins(every_bin, col0, True)
    fc[...] = picked[0:64]
    fine_c[...] = picked[64:128].astype(BF)
    w1 = weights[0].reshape(192, 192)
    w2 = weights[1].reshape(192, 192)
    cols = col0 + column_offsets((64, 256))
    in_cols = (cols >= 0) & (cols < SIDE)
    half_c, half_r = lax.rem(c, COLS // 2) * TC, lax.rem(r, ROWS // 2) * TR
    cols_q = half_c + column_offsets((64, 256))
    in_quarter = (cols_q >= 0) & (cols_q < SIDE // 2)
    low_half = lanes_of((64, 128)) < 64

    def pair_row(q, k, at, body, shift):
        rim = jnp.where(
            low_half,
            pltpu.roll(rim_right[q], (128 - 16 * k) % 128, 1),
            pltpu.roll(rim_left[q], 112 - 16 * k, 1),
        )
        prior = jnp.concatenate([body, rim], axis=1).astype(F32)
        value = prior + (fc[...] + shift[:, k : k + 1])
        grow = row0 + 8 * q + k - 16
        inside = in_cols & (grow >= 0) & (grow < SIDE)
        x[at] = jnp.where(inside, value, 0.0).astype(BF)

    def features_at(q):
        return pltpu.roll(fr[...], lax.rem(248 - 8 * q, 128), 1)

    def rim_rows(side):
        for k in range(10):
            row = 64 + k if side else k - 10
            q = (row + 16) // 8
            pair_row(q, row % 8, row + 10, rows[side, k], features_at(q))

    def own_rows(g):
        shift = features_at(g + 2)
        for k in range(8):
            pair_row(g + 2, k, 8 * g + k + 10, tile[8 * g + k], shift)

    def hidden_rows(first, taken, count):
        for t in range(count):
            at = first + t
            grow = row0 + at - 8
            value = jnp.maximum(tap_sum(taps1, taken + t, 2, 256) + bias[0], 0.0)
            inside = in_cols & (grow >= 0) & (grow < SIDE)
            hidden[at] = jnp.where(inside, value, 0.0).astype(BF)

    def field_rows(first, taken, count):
        for t in range(count):
            at = first + t
            qrow = half_r + at - 4
            value = jnp.maximum(tap_sum(taps2, taken + t, 4, 256) + bias[1], 0.0)
            inside = in_quarter & (qrow >= 0) & (qrow < SIDE // 2)
            fields[at] = jnp.where(inside, value, 0.0).astype(BF)

    def pack(j):
        t, q = j // 2, lax.rem(j, 2)
        for k in range(0, 16, 2):
            v = tap_sum(taps3, k, 4, 128).astype(BF)
            u = tap_sum(taps3, k + 1, 4, 128).astype(BF)
            at = 8 * q + k // 2
            pieces[0, t, at] = jnp.where(low_half, v, pltpu.roll(u, 64, 1))
            pieces[1, t, at] = jnp.where(low_half, pltpu.roll(v, 64, 1), u)

    for y in first + second:
        y.wait_send()
    for y, out, into in outlines:
        pl.when(out)(y.wait_send)
        pl.when(into)(y.wait_recv)
    rim_rows(0)

    def early_rows(g, carry):
        own_rows(g)
        return carry

    lax.fori_loop(0, 4, early_rows, 0)
    tap_products(w1, x, 0, taps1, 0, 20, 10, 2, 256)
    hidden_rows(0, 0, 16)
    tap_products(w2, hidden, 0, taps2, 8, 16, 8, 4, 256)
    field_rows(0, 8, 8)
    tap_products(w3[...], fields, 0, taps3, 16, 8, 8, 4, 128)
    def chunk(j, carry):
        @pl.when((j == 1) | (j == 2))
        def _():
            own_rows(2 * j + 2)
            own_rows(2 * j + 3)

        pl.when(j == 3)(lambda: rim_rows(1))
        carry_taps(taps1, 2)
        carry_taps(taps2, 4)
        carry_taps(taps3, 4)
        tap_products(w1, x, 20 + 16 * j, taps1, 4, 16, 8, 2, 256)
        hidden_rows(16 + 16 * j, 0, 16)
        tap_products(w2, hidden, 16 + 16 * j, taps2, 8, 16, 8, 4, 256)
        field_rows(8 + 16 * j, 0, 16)
        tap_products(w3[...], fields, 8 + 16 * j, taps3, 8, 16, 8, 4, 128)
        pack(j)
        for k in range(2):
            pl.when(is_source & away(main_to(j // 2, k)))(lambda k=k: piece(j, k).start())
            pl.when(is_source & jnp.logical_not(away(main_to(j // 2, k))))(
                lambda k=k: stay(j, k).start()
            )
        return carry

    lax.fori_loop(0, 4, chunk, 0)
    for q in range(4):
        map_out[:, 16 * q : 16 * q + 16, :] = jnp.swapaxes(
            fields[4 + 16 * q : 20 + 16 * q, :, 0:128], 0, 1
        )

    store_map = pltpu.make_async_copy(map_out, map_result, load.at[0])
    store_map.start()

    wq = halves_joined(joined[:, 0:128], joined[:, 128:256], joined[:, 256:384], True)
    wp = jnp.concatenate(
        [
            halves_joined(*[first_refine[a, :, 128 * e : 128 * e + 128] for a in range(3)], True)
            for e in range(3)
        ],
        axis=0,
    )
    w4 = second_refine[...].reshape(192, 192)
    terms = jnp.dot(wq, shifted_stack(fine_c[...], 8, 256), preferred_element_type=F32)
    base = terms[64:128] + bias_columns(refine_bias, 0, 256)
    row_terms[0] = base + terms[0:64] + terms[128:192]
    row_terms[1] = base + terms[128:192]
    row_terms[2] = base + terms[0:64]
    stack = jnp.concatenate([pltpu.roll(fine_r[...], 8, 1), fine_r[...], pltpu.roll(fine_r[...], 120, 1)], axis=0)
    terms = jnp.dot(wp, stack, preferred_element_type=F32)
    row_part[0] = terms[0:64] + terms[64:128] + terms[128:192]
    row_part[1] = terms[64:128] + jnp.where(c == 0, terms[128:192], terms[0:64])
    bias[0] = bias_columns(refine_bias, 1, 256)

    def spread_main(source, first, count, at):
        for k in range(2):
            value = jnp.dot(
                source[first : first + count].reshape(count * 64, 128),
                main_table[k],
                preferred_element_type=F32,
            )
            wide[at : at + count, k, :, 0:128] = value.reshape(count, 64, 128).astype(BF)

    part = lanes_of((64, 128)) // 8
    for q in range(2):
        pl.when(remote_main)(lambda: piece(q, 0).wait_recv())
        pl.when(jnp.logical_not(remote_main))(lambda: stay(q, 0).wait())
        low = high = None
        for k in range(16):
            v = got[8 * q + k // 2]
            first = (8 * k - 64 * (k % 2)) % 128
            moved, other = pltpu.roll(v, first, 1), pltpu.roll(v, (first - 56) % 128, 1)
            low = moved if k == 0 else jnp.where(part == k, moved, low)
            high = other if k == 0 else jnp.where(part == k, other, high)
        sides[0, q] = low
        sides[1, q] = high
    rims = [
        (got.at[pl.ds(12, 4)], top, (down, c), has_down, has_up),
        (got.at[pl.ds(0, 4)], bottom, (up, c), has_up, has_down),
        (sides.at[0], side_in.at[1, pl.ds(1, 2)], (r, west), has_west, has_east),
        (sides.at[1], side_in.at[0, pl.ds(1, 2)], (r, east), has_east, has_west),
        (sides.at[0, 1], side_in.at[1, 0], (down, west),
         has_down & has_west, has_up & has_east),
        (sides.at[1, 1], side_in.at[0, 0], (down, east),
         has_down & has_east, has_up & has_west),
        (sides.at[0, 0], side_in.at[1, 3], (up, west),
         has_up & has_west, has_down & has_east),
        (sides.at[1, 0], side_in.at[0, 3], (up, east),
         has_up & has_east, has_down & has_west),
    ]
    rims = [
        (copy(s, t, send_n.at[k], recv_n.at[k], to), out, into)
        for k, (s, t, to, out, into) in enumerate(rims)
    ]
    for y, out, _ in rims:
        pl.when(out)(y.start)

    offsets = column_offsets((64, 256)) + col0
    inside_of = [(offsets >= 0) & (offsets < SIDE)]
    edge_of = [(offsets < 8) | (offsets >= SIDE - 8)]

    def fine_rows(g, at):
        lanes = slice(at, at + 128)
        grow0 = row0 + 8 * g - 16
        inside = inside_of[0][:, lanes] & (grow0 >= 0) & (grow0 < SIDE)
        variant = jnp.where(grow0 == 0, 1, jnp.where(grow0 == SIDE - 8, 2, 0))
        shift = lax.rem(256 - 8 * g - 8, 128)
        everywhere = pltpu.roll(row_part[0], shift, 1)
        edge = pltpu.roll(row_part[1], shift, 1)
        column_terms = row_terms[variant, :, lanes]
        for k in range(8):
            row = jnp.where(edge_of[0][:, lanes], edge[:, k : k + 1], everywhere[:, k : k + 1])
            value = wide[2 * g + k // 4, (k // 2) % 2, :, lanes].astype(F32) + (column_terms + row)
            fine[8 * g + k, :, lanes] = jnp.where(inside, jnp.maximum(value, 0.0), 0.0).astype(BF)

    def own_fine_rows(g, carry):
        fine_rows(g, 0)
        return carry

    def side_fine_rows(g, carry):
        fine_rows(g, 128)
        return carry

    spread_main(got, 0, 16, 4)
    lax.fori_loop(2, 10, own_fine_rows, 0)
    for j in range(4):
        for k in range(2):
            pl.when(is_source & away(main_to(j // 2, k)))(lambda: piece(j, k).wait_send())
    for y, out, into in rims:
        pl.when(out)(y.wait_send)
        pl.when(into)(y.wait_recv)
    spread_main(top, 0, 4, 0)
    spread_main(bottom, 0, 4, 20)

    def spread_rim(tile_at, low, high, first):
        both = jnp.concatenate(
            [
                jnp.where(has_east, side_in[1, tile_at].astype(F32), 0.0),
                jnp.where(has_west, side_in[0, tile_at].astype(F32), 0.0),
            ],
            axis=1,
        ).astype(BF)
        value = jnp.dot(
            both, rim_table[:, 128 * low : 128 * high], preferred_element_type=F32
        ).astype(BF)
        for k in range(high - low):
            row = first + k
            wide[row // 2, row % 2, :, 128:256] = value[:, 128 * k : 128 * k + 128]

    spread_rim(0, 8, 16, 0)
    spread_rim(1, 0, 16, 8)
    spread_rim(2, 0, 16, 24)
    spread_rim(3, 0, 8, 40)
    for g in (0, 1, 10, 11):
        fine_rows(g, 0)
    lax.fori_loop(0, 12, side_fine_rows, 0)

    def last_products(g, carry):
        tap_products(w4, fine, 16 * g, taps4, 16 * g, 16, 8, 16, 128)
        return carry

    lax.fori_loop(0, 6, last_products, 0)
    for g in range(4):
        value = jnp.stack(
            [
                jnp.maximum(tap_sum(taps4, 16 * g + k, 16, 128) + bias[0, :, 0:128], 0.0).astype(BF)
                for k in range(16)
            ]
        )
        refined[:, 16 * g : 16 * g + 16, :] = jnp.swapaxes(value, 0, 1)
    store_refined = pltpu.make_async_copy(refined, refined_result, load.at[1])
    store_refined.start()
    store_map.wait()
    store_refined.wait()


def decoder(half, *arguments):
    return pl.pallas_call(
        functools.partial(decoder_kernel, half),
        out_shape=(
            jax.ShapeDtypeStruct((64, TR, TC), BF),
            jax.ShapeDtypeStruct((64, TR, TC), BF),
        ),
        in_specs=[anywhere] * 10,
        out_specs=(anywhere, anywhere),
        scratch_shapes=[
            pltpu.VMEM((64, TR, TC), BF),
            pltpu.VMEM((2, 3, 64, 192), BF),
            pltpu.VMEM((3, 64, 384), BF),
            pltpu.VMEM((3, 64, 192), BF),
            pltpu.VMEM((2, 64), F32),
            pltpu.VMEM((2, 64), F32),
            pltpu.VMEM((2, 128, 128), BF),
            pltpu.VMEM((256, 2048), BF),
            pltpu.VMEM((TR, 64, TC), BF),
            pltpu.VMEM((2, 10, 64, TC), BF),
            pltpu.VMEM((12, 64, TC), BF),
            pltpu.VMEM((12, 64, TC), BF),
            pltpu.VMEM((8, 64, TC), BF),
            pltpu.VMEM((8, 64, TC), BF),
            pltpu.VMEM((2, 8, 64), BF),
            pltpu.VMEM((ROWS * COLS, 8, TC), BF),
            pltpu.VMEM((64, TR, TC), BF),
            pltpu.VMEM((64, TR, TC), BF),
            pltpu.VMEM((84, 64, 256), BF),
            pltpu.VMEM((20, 192, 256), F32),
            pltpu.VMEM((80, 64, 256), BF),
            pltpu.VMEM((24, 192, 256), F32),
            pltpu.VMEM((72, 64, 256), BF),
            pltpu.VMEM((24, 192, 128), F32),
            pltpu.VMEM((192, 192), BF),
            pltpu.VMEM((2, 64, 256), F32),
            pltpu.VMEM((64, 128), F32),
            pltpu.VMEM((64, 256), F32),
            pltpu.VMEM((64, 128), BF),
            pltpu.VMEM((64, 256), BF),
            pltpu.VMEM((2, 2, 16, 64, 128), BF),
            pltpu.VMEM((16, 64, 128), BF),
            pltpu.VMEM((2, 2, 64, 128), BF),
            pltpu.VMEM((4, 64, 128), BF),
            pltpu.VMEM((4, 64, 128), BF),
            pltpu.VMEM((2, 4, 64, 128), BF),
            pltpu.VMEM((24, 2, 64, 256), BF),
            pltpu.VMEM((96, 64, 256), BF),
            pltpu.VMEM((96, 192, 128), F32),
            pltpu.VMEM((3, 64, 256), F32),
            pltpu.VMEM((2, 64, 128), F32),
            pltpu.SemaphoreType.DMA((8,)),
            pltpu.SemaphoreType.DMA((2,)),
            pltpu.SemaphoreType.DMA((2,)),
            pltpu.SemaphoreType.DMA((8,)),
            pltpu.SemaphoreType.DMA((8,)),
            pltpu.SemaphoreType.DMA((10,)),
            pltpu.SemaphoreType.DMA((8,)),
            pltpu.SemaphoreType.DMA((8,)),
            pltpu.SemaphoreType.DMA((COLS,)),
            pltpu.SemaphoreType.DMA((COLS,)),
            pltpu.SemaphoreType.DMA((ROWS,)),
            pltpu.SemaphoreType.DMA((ROWS,)),
        ],
        compiler_params=pltpu.CompilerParams(
            collective_id=2 + half, has_side_effects=True, vmem_limit_bytes=VMEM_BYTES
        ),
    )(*arguments)


def per_device(coarse_feats, fine_feats, pair_prior, zoom_start, coarse_weights, coarse_bias,
               refine_first, refine_second, refine_bias):
    main_table, rim_table = spread_tables()
    return lax.cond(
        zoom_start[0] == 0,
        functools.partial(decoder, 0),
        functools.partial(decoder, 1),
        coarse_feats.T, fine_feats.T, pair_prior, coarse_weights, refine_first, refine_second,
        coarse_bias, refine_bias, jnp.asarray(main_table, BF), jnp.asarray(rim_table, BF),
    )


def solution(mesh):
    return jax.shard_map(
        per_device,
        mesh=mesh,
        in_specs=(
            P(None, ("row", "col")),
            P(None, ("row", "col")),
            P(None, "row", "col"),
            P(),
            P(),
            P(),
            P(),
            P(),
            P(),
        ),
        out_specs=(P(None, "row", "col"), P(None, "row", "col")),
        check_vma=False,
    )
```

```python
import functools

import jax
import jax.numpy as jnp
import numpy as np
from jax import lax
from jax.experimental import pallas as pl
from jax.experimental.pallas import tpu as pltpu
from jax.sharding import PartitionSpec as P

BF = jnp.bfloat16
F32 = jnp.float32
MESH = pl.DeviceIdType.MESH
VMEM_BYTES = 58 << 20
SIDE = 1024
ROWS, COLS = 16, 8
TR, TC = 64, 128

anywhere = pl.BlockSpec(memory_space=pl.ANY)


def lanes_of(shape):
    return lax.broadcasted_iota(jnp.int32, shape, len(shape) - 1)


def column_offsets(shape):
    lane = lanes_of(shape)
    return jnp.where(lane < 192, lane, lane - 256)


def shifted_stack(x, spacing, width):
    return jnp.concatenate(
        [
            pltpu.roll(x, spacing, 1)[:, :width],
            x[:, :width],
            pltpu.roll(x, 256 - spacing, 1)[:, :width],
        ],
        axis=0,
    )


def tap_products(w, source, first, target, into, count, group, spacing, width):
    for g in range(count // group):
        base = first + g * group
        stack = jnp.concatenate(
            [shifted_stack(source[base + t], spacing, width) for t in range(group)], axis=1
        )
        product = jnp.dot(w, stack, preferred_element_type=F32)
        for t in range(group):
            target[into + g * group + t] = product[:, t * width : (t + 1) * width]


def carry_taps(target, spacing):
    for t in range(2 * spacing):
        last = target.shape[0] - 2 * spacing + t
        target[last - 8, 0:64] = target[last, 0:64]
        if t >= spacing:
            target[last - 8, 64:128] = target[last, 64:128]


def tap_sum(target, i, spacing, width):
    return (
        target[i, 0:64, 0:width]
        + target[i + spacing, 64:128, 0:width]
        + target[i + 2 * spacing, 128:192, 0:width]
    )


def bias_columns(bias, layer, width):
    row = jnp.broadcast_to(bias[layer : layer + 1, :], (128, 64))
    column = jnp.transpose(row)
    return column if width == 128 else jnp.concatenate([column, column], axis=1)


def halves_joined(a, b, c, upper):
    low = lanes_of(a.shape) < 64
    if upper:
        first = jnp.where(low, pltpu.roll(a, 64, 1), b)
        return jnp.concatenate([first, pltpu.roll(c, 64, 1)[:, :64]], axis=1)
    first = jnp.where(low, a, pltpu.roll(b, 64, 1))
    return jnp.concatenate([first, c[:, :64]], axis=1)


def chosen_bins(gathered, first, ring):
    lanes = 256 if ring else 128
    shape = (SIDE, lanes)
    wanted = first + (column_offsets(shape) if ring else lanes_of(shape))
    picked = lax.broadcasted_iota(jnp.int32, shape, 0) == wanted
    return lax.dot_general(
        gathered,
        jnp.where(picked, 1.0, 0.0).astype(BF),
        (((0,), (0,)), ((), ())),
        preferred_element_type=F32,
    )


def spread_tables():
    lane = np.arange(128)
    source = np.arange(128)[:, None]
    main = np.stack([source == 64 * k + lane[None] // 2 for k in range(2)])
    rim = np.zeros((256, 16, 128), bool)
    for k in range(16):
        rim[:128, k] = (source == 8 * k + lane[None] // 2) & (lane[None] < 16)
        rim[128:, k] = (source == 8 * k + (lane[None] - 112) // 2) & (lane[None] >= 112)
    return main.astype(np.float32), rim.reshape(256, 2048).astype(np.float32)


def decoder_kernel(half, coarse_feats, fine_feats, prior, coarse_weights, first_weights,
                   second_weights, coarse_biases, refine_biases, tables_main, tables_rim,
                   map_result, refined_result,
                   whole, weights, first_refine, second_refine, coarse_bias, refine_bias,
                   main_table, rim_table,
                   tile, rows, rim_left, rim_right, left, right, feats, gathered, map_out, refined,
                   x, taps1, hidden, taps2, fields, taps3, w3, bias, fr, fc, fine_r, fine_c, pieces,
                   got, sides, top, bottom, side_in, wide, fine, taps4, row_terms, row_part,
                   send, recv, own, send_n, recv_n,
                   load, send_f, recv_f, send_a, recv_a, send_b, recv_b):
    loads = [
        (prior, whole),
        (coarse_feats, feats.at[0]),
        (fine_feats, feats.at[1]),
        (coarse_weights, weights),
        (first_weights, first_refine),
        (second_weights, second_refine),
        (coarse_biases, coarse_bias),
        (refine_biases, refine_bias),
        (tables_main, main_table),
        (tables_rim, rim_table),
    ]
    loads = [pltpu.make_async_copy(s, d, load.at[k]) for k, (s, d) in enumerate(loads)]
    for y in loads:
        y.start()
    r, c = lax.axis_index("row"), lax.axis_index("col")
    base_r, base_c = half * (ROWS // 2), half * (COLS // 2)
    up, down = lax.rem(r + ROWS - 1, ROWS), lax.rem(r + 1, ROWS)
    west, east = lax.rem(c + COLS - 1, COLS), lax.rem(c + 1, COLS)
    has_up, has_down, has_west, has_east = r > 0, r < ROWS - 1, c > 0, c < COLS - 1
    from_r, from_c = base_r + r // 2, base_c + c // 2
    remote_main = (from_r != r) | (from_c != c)
    is_source = (r >= base_r) & (r < base_r + ROWS // 2) & (c >= base_c) & (c < base_c + COLS // 2)
    local_r, local_c = r - base_r, c - base_c

    def main_to(t, h):
        return 2 * local_r + t, 2 * local_c + h

    def away(to):
        return (to[0] != r) | (to[1] != c)

    gathered[...] = jnp.zeros(gathered.shape, BF)
    barrier = pltpu.get_barrier_semaphore()

    def greet(to):
        pl.semaphore_signal(barrier, 1, device_id=to, device_id_type=MESH)

    around = [
        ((up, c), has_up),
        ((down, c), has_down),
        ((r, west), has_west),
        ((r, east), has_east),
        ((up, west), has_up & has_west),
        ((up, east), has_up & has_east),
        ((down, west), has_down & has_west),
        ((down, east), has_down & has_east),
    ]
    met = around[4:] + [((from_r, from_c), remote_main)]
    met += [(main_to(t, k), is_source & away(main_to(t, k))) for t in range(2) for k in range(2)]
    for d in range(1, COLS):
        greet((r, lax.rem(c + d, COLS)))
    peers = COLS - 1

    def gives(a, b):
        return ((a >= 2 * c - 1) & (a <= 2 * c + 2)) | (a == b + 1) | (a == b - 1)

    for d in range(1, ROWS):
        other = lax.rem(r + d, ROWS)
        there = gives(r, other) | gives(other, r)
        pl.when(there)(functools.partial(greet, (other, c)))
        peers = peers + jnp.where(there, 1, 0)
    for to, there in met:
        pl.when(there)(functools.partial(greet, to))
        peers = peers + jnp.where(there, 1, 0)

    def copy(source, target, out_sem, in_sem, to):
        return pltpu.make_async_remote_copy(
            src_ref=source,
            dst_ref=target,
            send_sem=out_sem,
            recv_sem=in_sem,
            device_id=to,
            device_id_type=MESH,
        )

    def piece(j, k):
        t, q = j // 4, lax.rem(j, 4)
        return copy(pieces.at[k, t, pl.ds(4 * q, 4)], got.at[pl.ds(4 * q, 4)],
                    send.at[2 * j + k], recv.at[q], main_to(t, k))

    def stay(j, k):
        t, q = j // 4, lax.rem(j, 4)
        return pltpu.make_async_copy(
            pieces.at[k, t, pl.ds(4 * q, 4)], got.at[pl.ds(4 * q, 4)], own.at[q]
        )

    for y in loads[1:3]:
        y.wait()
    place = r * COLS + c
    gathered[place] = jnp.concatenate([feats[0], feats[1]], axis=1)
    pl.semaphore_wait(barrier, peers)
    first = [
        copy(gathered.at[place], gathered.at[place], send_a.at[d], recv_a.at[d],
             (r, lax.rem(c + d, COLS)))
        for d in range(1, COLS)
    ]
    for y in first:
        y.start()
    loads[0].wait()
    for q in range(4):
        tile[16 * q : 16 * q + 16] = jnp.swapaxes(whole[:, 16 * q : 16 * q + 16, :], 0, 1)
    sixteenth = lanes_of((64, 128)) // 16

    def pack_edges(q, carry):
        low = tile[8 * q]
        high = pltpu.roll(low, 16, 1)
        for k in range(1, 8):
            v = tile[8 * q + k]
            low = jnp.where(sixteenth == k, pltpu.roll(v, 16 * k, 1), low)
            high = jnp.where(sixteenth == k, pltpu.roll(v, (16 * k + 16) % 128, 1), high)
        left[q] = low
        right[q] = high
        return carry

    lax.fori_loop(0, 8, pack_edges, 0)
    outlines = [
        (right, rim_left.at[pl.ds(2, 8)], (r, east), has_east, has_west),
        (left, rim_right.at[pl.ds(2, 8)], (r, west), has_west, has_east),
        (tile.at[pl.ds(54, 10)], rows.at[0], (down, c), has_down, has_up),
        (tile.at[pl.ds(0, 10)], rows.at[1], (up, c), has_up, has_down),
        (right.at[pl.ds(6, 2)], rim_left.at[pl.ds(0, 2)], (down, east),
         has_down & has_east, has_up & has_west),
        (right.at[pl.ds(0, 2)], rim_left.at[pl.ds(10, 2)], (up, east),
         has_up & has_east, has_down & has_west),
        (left.at[pl.ds(6, 2)], rim_right.at[pl.ds(0, 2)], (down, west),
         has_down & has_west, has_up & has_east),
        (left.at[pl.ds(0, 2)], rim_right.at[pl.ds(10, 2)], (up, west),
         has_up & has_west, has_down & has_east),
    ]
    outlines = [
        (copy(s, t, send_f.at[k], recv_f.at[k], to), out, into)
        for k, (s, t, to, out, into) in enumerate(outlines)
    ]
    for y, out, _ in outlines:
        pl.when(out)(y.start)
    for y in first:
        y.wait_recv()
    block = gathered.at[pl.ds(r * COLS, COLS)]
    second = [
        copy(block, block, send_b.at[d], recv_b.at[d], (lax.rem(r + d, ROWS), c))
        for d in range(1, ROWS)
    ]
    for d, y in enumerate(second, 1):
        pl.when(gives(r, lax.rem(r + d, ROWS)))(y.start)
    for y in loads[3:]:
        y.wait()
    joined = first_refine[...].reshape(192, 384)
    w3[...] = halves_joined(joined[:, 0:128], joined[:, 128:256], joined[:, 256:384], False)
    bias[0] = bias_columns(coarse_bias, 0, 256)
    bias[1] = bias_columns(coarse_bias, 1, 256)
    for d, y in enumerate(second, 1):
        pl.when(gives(lax.rem(r + ROWS - d, ROWS), r))(y.wait_recv)

    row0, col0 = r * TR, c * TC
    every_bin = gathered[...].reshape(SIDE, 128)
    picked = chosen_bins(every_bin, row0 - 24, False)
    fr[...] = picked[0:64]
    fine_r[...] = picked[64:128].astype(BF)
    picked = chosen_bins(every_bin, col0, True)
    fc[...] = picked[0:64]
    fine_c[...] = picked[64:128].astype(BF)
    w1 = weights[0].reshape(192, 192)
    w2 = weights[1].reshape(192, 192)
    cols = col0 + column_offsets((64, 256))
    in_cols = (cols >= 0) & (cols < SIDE)
    half_c, half_r = lax.rem(c, COLS // 2) * TC, lax.rem(r, ROWS // 2) * TR
    cols_q = half_c + column_offsets((64, 256))
    in_quarter = (cols_q >= 0) & (cols_q < SIDE // 2)
    low_half = lanes_of((64, 128)) < 64

    def pair_row(q, k, at, body, shift):
        rim = jnp.where(
            low_half,
            pltpu.roll(rim_right[q], (128 - 16 * k) % 128, 1),
            pltpu.roll(rim_left[q], 112 - 16 * k, 1),
        )
        prior = jnp.concatenate([body, rim], axis=1).astype(F32)
        value = prior + (fc[...] + shift[:, k : k + 1])
        grow = row0 + 8 * q + k - 16
        inside = in_cols & (grow >= 0) & (grow < SIDE)
        x[at] = jnp.where(inside, value, 0.0).astype(BF)

    def features_at(q):
        return pltpu.roll(fr[...], lax.rem(248 - 8 * q, 128), 1)

    def rim_rows(side):
        for k in range(10):
            row = 64 + k if side else k - 10
            q = (row + 16) // 8
            pair_row(q, row % 8, row + 10, rows[side, k], features_at(q))

    def own_rows(g):
        shift = features_at(g + 2)
        for k in range(8):
            pair_row(g + 2, k, 8 * g + k + 10, tile[8 * g + k], shift)

    def hidden_rows(first, taken, count):
        for t in range(count):
            at = first + t
            grow = row0 + at - 8
            value = jnp.maximum(tap_sum(taps1, taken + t, 2, 256) + bias[0], 0.0)
            inside = in_cols & (grow >= 0) & (grow < SIDE)
            hidden[at] = jnp.where(inside, value, 0.0).astype(BF)

    def field_rows(first, taken, count):
        for t in range(count):
            at = first + t
            qrow = half_r + at - 4
            value = jnp.maximum(tap_sum(taps2, taken + t, 4, 256) + bias[1], 0.0)
            inside = in_quarter & (qrow >= 0) & (qrow < SIDE // 2)
            fields[at] = jnp.where(inside, value, 0.0).astype(BF)

    def pack(j):
        t, q = j // 4, lax.rem(j, 4)
        for k in range(0, 8, 2):
            v = tap_sum(taps3, k, 4, 128).astype(BF)
            u = tap_sum(taps3, k + 1, 4, 128).astype(BF)
            at = 4 * q + k // 2
            pieces[0, t, at] = jnp.where(low_half, v, pltpu.roll(u, 64, 1))
            pieces[1, t, at] = jnp.where(low_half, pltpu.roll(v, 64, 1), u)

    for y in first:
        y.wait_send()
    for d, y in enumerate(second, 1):
        pl.when(gives(r, lax.rem(r + d, ROWS)))(y.wait_send)
    for y, out, into in outlines:
        pl.when(out)(y.wait_send)
        pl.when(into)(y.wait_recv)
    rim_rows(0)

    def early_rows(g, carry):
        own_rows(g)
        return carry

    lax.fori_loop(0, 2, early_rows, 0)
    tap_products(w1, x, 0, taps1, 0, 20, 10, 2, 256)
    hidden_rows(0, 0, 16)
    tap_products(w2, hidden, 0, taps2, 0, 16, 8, 4, 256)
    field_rows(0, 0, 8)
    tap_products(w3[...], fields, 0, taps3, 8, 8, 8, 4, 128)
    def chunk(j, carry):
        pl.when(j < 6)(lambda: own_rows(j + 2))
        pl.when(j == 6)(lambda: rim_rows(1))
        carry_taps(taps1, 2)
        carry_taps(taps2, 4)
        carry_taps(taps3, 4)
        tap_products(w1, x, 20 + 8 * j, taps1, 12, 8, 8, 2, 256)
        hidden_rows(16 + 8 * j, 8, 8)
        tap_products(w2, hidden, 16 + 8 * j, taps2, 8, 8, 8, 4, 256)
        field_rows(8 + 8 * j, 0, 8)
        tap_products(w3[...], fields, 8 + 8 * j, taps3, 8, 8, 8, 4, 128)
        pack(j)
        for k in range(2):
            pl.when(is_source & away(main_to(j // 4, k)))(lambda k=k: piece(j, k).start())
            pl.when(is_source & jnp.logical_not(away(main_to(j // 4, k))))(
                lambda k=k: stay(j, k).start()
            )
        return carry

    lax.fori_loop(0, 8, chunk, 0)
    for q in range(4):
        map_out[:, 16 * q : 16 * q + 16, :] = jnp.swapaxes(
            fields[4 + 16 * q : 20 + 16 * q, :, 0:128], 0, 1
        )

    store_map = pltpu.make_async_copy(map_out, map_result, load.at[0])
    store_map.start()

    wq = halves_joined(joined[:, 0:128], joined[:, 128:256], joined[:, 256:384], True)
    wp = jnp.concatenate(
        [
            halves_joined(*[first_refine[a, :, 128 * e : 128 * e + 128] for a in range(3)], True)
            for e in range(3)
        ],
        axis=0,
    )
    w4 = second_refine[...].reshape(192, 192)
    terms = jnp.dot(wq, shifted_stack(fine_c[...], 8, 256), preferred_element_type=F32)
    base = terms[64:128] + bias_columns(refine_bias, 0, 256)
    row_terms[0] = base + terms[0:64] + terms[128:192]
    row_terms[1] = base + terms[128:192]
    row_terms[2] = base + terms[0:64]
    stack = jnp.concatenate([pltpu.roll(fine_r[...], 8, 1), fine_r[...], pltpu.roll(fine_r[...], 120, 1)], axis=0)
    terms = jnp.dot(wp, stack, preferred_element_type=F32)
    row_part[0] = terms[0:64] + terms[64:128] + terms[128:192]
    row_part[1] = terms[64:128] + jnp.where(c == 0, terms[128:192], terms[0:64])
    bias[0] = bias_columns(refine_bias, 1, 256)

    def spread_main(source, first, count, at):
        for k in range(2):
            value = jnp.dot(
                source[first : first + count].reshape(count * 64, 128),
                main_table[k],
                preferred_element_type=F32,
            )
            wide[at : at + count, k, :, 0:128] = value.reshape(count, 64, 128).astype(BF)

    rims = [
        (got.at[pl.ds(0, 4)], bottom, (up, c), has_up, has_down, 0),
        (sides.at[0, 0], side_in.at[1, 1], (r, west), has_west, has_east, 1),
        (sides.at[1, 0], side_in.at[0, 1], (r, east), has_east, has_west, 1),
        (sides.at[0, 0], side_in.at[1, 3], (up, west),
         has_up & has_west, has_down & has_east, 1),
        (sides.at[1, 0], side_in.at[0, 3], (up, east),
         has_up & has_east, has_down & has_west, 1),
        (got.at[pl.ds(12, 4)], top, (down, c), has_down, has_up, 3),
        (sides.at[0, 1], side_in.at[1, 2], (r, west), has_west, has_east, 3),
        (sides.at[1, 1], side_in.at[0, 2], (r, east), has_east, has_west, 3),
        (sides.at[0, 1], side_in.at[1, 0], (down, west),
         has_down & has_west, has_up & has_east, 3),
        (sides.at[1, 1], side_in.at[0, 0], (down, east),
         has_down & has_east, has_up & has_west, 3),
    ]
    rims = [
        (copy(s, t, send_n.at[k], recv_n.at[k], to), out, into, when)
        for k, (s, t, to, out, into, when) in enumerate(rims)
    ]
    part = lanes_of((64, 128)) // 8

    def pack_sides(half_tile):
        low = high = None
        for k in range(16):
            v = got[8 * half_tile + k // 2]
            start = (8 * k - 64 * (k % 2)) % 128
            moved, other = pltpu.roll(v, start, 1), pltpu.roll(v, (start - 56) % 128, 1)
            low = moved if k == 0 else jnp.where(part == k, moved, low)
            high = other if k == 0 else jnp.where(part == k, other, high)
        sides[0, half_tile] = low
        sides[1, half_tile] = high

    offsets = column_offsets((64, 256)) + col0
    inside_of = [(offsets >= 0) & (offsets < SIDE)]
    edge_of = [(offsets < 8) | (offsets >= SIDE - 8)]

    def fine_rows(g, at):
        lanes = slice(at, at + 128)
        grow0 = row0 + 8 * g - 16
        inside = inside_of[0][:, lanes] & (grow0 >= 0) & (grow0 < SIDE)
        variant = jnp.where(grow0 == 0, 1, jnp.where(grow0 == SIDE - 8, 2, 0))
        shift = lax.rem(256 - 8 * g - 8, 128)
        everywhere = pltpu.roll(row_part[0], shift, 1)
        edge = pltpu.roll(row_part[1], shift, 1)
        column_terms = row_terms[variant, :, lanes]
        for k in range(8):
            row = jnp.where(edge_of[0][:, lanes], edge[:, k : k + 1], everywhere[:, k : k + 1])
            value = wide[2 * g + k // 4, (k // 2) % 2, :, lanes].astype(F32) + (column_terms + row)
            fine[8 * g + k, :, lanes] = jnp.where(inside, jnp.maximum(value, 0.0), 0.0).astype(BF)

    def own_fine_rows(g, carry):
        fine_rows(g, 0)
        return carry

    def side_fine_rows(g, carry):
        fine_rows(g, 128)
        return carry

    for q in range(4):
        pl.when(remote_main)(lambda: piece(q, 0).wait_recv())
        pl.when(jnp.logical_not(remote_main))(lambda: stay(q, 0).wait())
        if q % 2:
            pack_sides(q // 2)
        for y, out, _, when in rims:
            if when == q:
                pl.when(out)(y.start)
        spread_main(got, 4 * q, 4, 4 + 4 * q)
        lax.fori_loop(2 + 2 * q, 4 + 2 * q, own_fine_rows, 0)
    for j in range(8):
        for k in range(2):
            pl.when(is_source & away(main_to(j // 4, k)))(lambda: piece(j, k).wait_send())
    for y, out, into, _ in rims:
        pl.when(out)(y.wait_send)
        pl.when(into)(y.wait_recv)
    spread_main(top, 0, 4, 0)
    spread_main(bottom, 0, 4, 20)

    def spread_rim(tile_at, low, high, first):
        both = jnp.concatenate(
            [
                jnp.where(has_east, side_in[1, tile_at].astype(F32), 0.0),
                jnp.where(has_west, side_in[0, tile_at].astype(F32), 0.0),
            ],
            axis=1,
        ).astype(BF)
        value = jnp.dot(
            both, rim_table[:, 128 * low : 128 * high], preferred_element_type=F32
        ).astype(BF)
        for k in range(high - low):
            row = first + k
            wide[row // 2, row % 2, :, 128:256] = value[:, 128 * k : 128 * k + 128]

    spread_rim(0, 8, 16, 0)
    spread_rim(1, 0, 16, 8)
    spread_rim(2, 0, 16, 24)
    spread_rim(3, 0, 8, 40)
    for g in (0, 1, 10, 11):
        fine_rows(g, 0)
    lax.fori_loop(0, 12, side_fine_rows, 0)

    def last_products(g, carry):
        tap_products(w4, fine, 16 * g, taps4, 16 * g, 16, 8, 16, 128)
        return carry

    lax.fori_loop(0, 6, last_products, 0)
    for g in range(4):
        value = jnp.stack(
            [
                jnp.maximum(tap_sum(taps4, 16 * g + k, 16, 128) + bias[0, :, 0:128], 0.0).astype(BF)
                for k in range(16)
            ]
        )
        refined[:, 16 * g : 16 * g + 16, :] = jnp.swapaxes(value, 0, 1)
    store_refined = pltpu.make_async_copy(refined, refined_result, load.at[1])
    store_refined.start()
    store_map.wait()
    store_refined.wait()


def decoder(half, *arguments):
    return pl.pallas_call(
        functools.partial(decoder_kernel, half),
        out_shape=(
            jax.ShapeDtypeStruct((64, TR, TC), BF),
            jax.ShapeDtypeStruct((64, TR, TC), BF),
        ),
        in_specs=[anywhere] * 10,
        out_specs=(anywhere, anywhere),
        scratch_shapes=[
            pltpu.VMEM((64, TR, TC), BF),
            pltpu.VMEM((2, 3, 64, 192), BF),
            pltpu.VMEM((3, 64, 384), BF),
            pltpu.VMEM((3, 64, 192), BF),
            pltpu.VMEM((2, 64), F32),
            pltpu.VMEM((2, 64), F32),
            pltpu.VMEM((2, 128, 128), BF),
            pltpu.VMEM((256, 2048), BF),
            pltpu.VMEM((TR, 64, TC), BF),
            pltpu.VMEM((2, 10, 64, TC), BF),
            pltpu.VMEM((12, 64, TC), BF),
            pltpu.VMEM((12, 64, TC), BF),
            pltpu.VMEM((8, 64, TC), BF),
            pltpu.VMEM((8, 64, TC), BF),
            pltpu.VMEM((2, 8, 64), BF),
            pltpu.VMEM((ROWS * COLS, 8, TC), BF),
            pltpu.VMEM((64, TR, TC), BF),
            pltpu.VMEM((64, TR, TC), BF),
            pltpu.VMEM((84, 64, 256), BF),
            pltpu.VMEM((20, 192, 256), F32),
            pltpu.VMEM((80, 64, 256), BF),
            pltpu.VMEM((16, 192, 256), F32),
            pltpu.VMEM((72, 64, 256), BF),
            pltpu.VMEM((16, 192, 128), F32),
            pltpu.VMEM((192, 192), BF),
            pltpu.VMEM((2, 64, 256), F32),
            pltpu.VMEM((64, 128), F32),
            pltpu.VMEM((64, 256), F32),
            pltpu.VMEM((64, 128), BF),
            pltpu.VMEM((64, 256), BF),
            pltpu.VMEM((2, 2, 16, 64, 128), BF),
            pltpu.VMEM((16, 64, 128), BF),
            pltpu.VMEM((2, 2, 64, 128), BF),
            pltpu.VMEM((4, 64, 128), BF),
            pltpu.VMEM((4, 64, 128), BF),
            pltpu.VMEM((2, 4, 64, 128), BF),
            pltpu.VMEM((24, 2, 64, 256), BF),
            pltpu.VMEM((96, 64, 256), BF),
            pltpu.VMEM((96, 192, 128), F32),
            pltpu.VMEM((3, 64, 256), F32),
            pltpu.VMEM((2, 64, 128), F32),
            pltpu.SemaphoreType.DMA((16,)),
            pltpu.SemaphoreType.DMA((4,)),
            pltpu.SemaphoreType.DMA((4,)),
            pltpu.SemaphoreType.DMA((10,)),
            pltpu.SemaphoreType.DMA((10,)),
            pltpu.SemaphoreType.DMA((10,)),
            pltpu.SemaphoreType.DMA((8,)),
            pltpu.SemaphoreType.DMA((8,)),
            pltpu.SemaphoreType.DMA((COLS,)),
            pltpu.SemaphoreType.DMA((COLS,)),
            pltpu.SemaphoreType.DMA((ROWS,)),
            pltpu.SemaphoreType.DMA((ROWS,)),
        ],
        compiler_params=pltpu.CompilerParams(
            collective_id=2 + half, has_side_effects=True, vmem_limit_bytes=VMEM_BYTES
        ),
    )(*arguments)


def per_device(coarse_feats, fine_feats, pair_prior, zoom_start, coarse_weights, coarse_bias,
               refine_first, refine_second, refine_bias):
    main_table, rim_table = spread_tables()
    return lax.cond(
        zoom_start[0] == 0,
        functools.partial(decoder, 0),
        functools.partial(decoder, 1),
        coarse_feats.T, fine_feats.T, pair_prior, coarse_weights, refine_first, refine_second,
        coarse_bias, refine_bias, jnp.asarray(main_table, BF), jnp.asarray(rim_table, BF),
    )


def solution(mesh):
    return jax.shard_map(
        per_device,
        mesh=mesh,
        in_specs=(
            P(None, ("row", "col")),
            P(None, ("row", "col")),
            P(None, "row", "col"),
            P(),
            P(),
            P(),
            P(),
            P(),
            P(),
        ),
        out_specs=(P(None, "row", "col"), P(None, "row", "col")),
        check_vma=False,
    )
```

```python
import functools

import jax
import jax.numpy as jnp
import numpy as np
from jax import lax
from jax.experimental import pallas as pl
from jax.experimental.pallas import tpu as pltpu
from jax.sharding import PartitionSpec as P

BF = jnp.bfloat16
F32 = jnp.float32
MESH = pl.DeviceIdType.MESH
VMEM_BYTES = 58 << 20
SIDE = 1024
ROWS, COLS = 16, 8
TR, TC = 64, 128

anywhere = pl.BlockSpec(memory_space=pl.ANY)


def lanes_of(shape):
    return lax.broadcasted_iota(jnp.int32, shape, len(shape) - 1)


def column_offsets(shape):
    lane = lanes_of(shape)
    return jnp.where(lane < 192, lane, lane - 256)


def shifted_stack(x, spacing, width):
    return jnp.concatenate(
        [
            pltpu.roll(x, spacing, 1)[:, :width],
            x[:, :width],
            pltpu.roll(x, 256 - spacing, 1)[:, :width],
        ],
        axis=0,
    )


def tap_products(w, source, first, target, into, count, group, spacing, width):
    for g in range(count // group):
        base = first + g * group
        stack = jnp.concatenate(
            [shifted_stack(source[base + t], spacing, width) for t in range(group)], axis=1
        )
        product = jnp.dot(w, stack, preferred_element_type=F32)
        for t in range(group):
            target[into + g * group + t] = product[:, t * width : (t + 1) * width]


def carry_taps(target, spacing):
    for t in range(2 * spacing):
        last = target.shape[0] - 2 * spacing + t
        target[last - 8, 0:64] = target[last, 0:64]
        if t >= spacing:
            target[last - 8, 64:128] = target[last, 64:128]


def tap_sum(target, i, spacing, width):
    return (
        target[i, 0:64, 0:width]
        + target[i + spacing, 64:128, 0:width]
        + target[i + 2 * spacing, 128:192, 0:width]
    )


def bias_columns(bias, layer, width):
    row = jnp.broadcast_to(bias[layer : layer + 1, :], (128, 64))
    column = jnp.transpose(row)
    return column if width == 128 else jnp.concatenate([column, column], axis=1)


def halves_joined(a, b, c, upper):
    low = lanes_of(a.shape) < 64
    if upper:
        first = jnp.where(low, pltpu.roll(a, 64, 1), b)
        return jnp.concatenate([first, pltpu.roll(c, 64, 1)[:, :64]], axis=1)
    first = jnp.where(low, a, pltpu.roll(b, 64, 1))
    return jnp.concatenate([first, c[:, :64]], axis=1)


def chosen_bins(gathered, first, ring):
    lanes = 256 if ring else 128
    shape = (SIDE, lanes)
    wanted = first + (column_offsets(shape) if ring else lanes_of(shape))
    picked = lax.broadcasted_iota(jnp.int32, shape, 0) == wanted
    return lax.dot_general(
        gathered,
        jnp.where(picked, 1.0, 0.0).astype(BF),
        (((0,), (0,)), ((), ())),
        preferred_element_type=F32,
    )


def spread_tables():
    lane = np.arange(128)
    source = np.arange(128)[:, None]
    main = np.stack([source == 64 * k + lane[None] // 2 for k in range(2)])
    rim = np.zeros((256, 16, 128), bool)
    for k in range(16):
        rim[:128, k] = (source == 8 * k + lane[None] // 2) & (lane[None] < 16)
        rim[128:, k] = (source == 8 * k + (lane[None] - 112) // 2) & (lane[None] >= 112)
    return main.astype(np.float32), rim.reshape(256, 2048).astype(np.float32)


def decoder_kernel(half, coarse_feats, fine_feats, prior, coarse_weights, first_weights,
                   second_weights, coarse_biases, refine_biases, tables_main, tables_rim,
                   map_result, refined_result,
                   whole, weights, first_refine, second_refine, coarse_bias, refine_bias,
                   main_table, rim_table,
                   tile, rows, rim_left, rim_right, left, right, feats, gathered, map_out, refined,
                   x, taps1, hidden, taps2, fields, taps3, w3, bias, fr, fc, fine_r, fine_c, pieces,
                   got, sides, top, bottom, side_in, wide, fine, taps4, row_terms, row_part,
                   send, recv, own, send_n, recv_n,
                   load, send_f, recv_f, send_a, recv_a, send_b, recv_b):
    loads = [
        (prior, whole),
        (coarse_feats, feats.at[0]),
        (fine_feats, feats.at[1]),
        (coarse_weights, weights),
        (first_weights, first_refine),
        (second_weights, second_refine),
        (coarse_biases, coarse_bias),
        (refine_biases, refine_bias),
        (tables_main, main_table),
        (tables_rim, rim_table),
    ]
    loads = [pltpu.make_async_copy(s, d, load.at[k]) for k, (s, d) in enumerate(loads)]
    for y in loads:
        y.start()
    r, c = lax.axis_index("row"), lax.axis_index("col")
    base_r, base_c = half * (ROWS // 2), half * (COLS // 2)
    up, down = lax.rem(r + ROWS - 1, ROWS), lax.rem(r + 1, ROWS)
    west, east = lax.rem(c + COLS - 1, COLS), lax.rem(c + 1, COLS)
    has_up, has_down, has_west, has_east = r > 0, r < ROWS - 1, c > 0, c < COLS - 1
    from_r, from_c = base_r + r // 2, base_c + c // 2
    remote_main = (from_r != r) | (from_c != c)
    is_source = (r >= base_r) & (r < base_r + ROWS // 2) & (c >= base_c) & (c < base_c + COLS // 2)
    local_r, local_c = r - base_r, c - base_c

    def main_to(t, h):
        return 2 * local_r + t, 2 * local_c + h

    def away(to):
        return (to[0] != r) | (to[1] != c)

    gathered[...] = jnp.zeros(gathered.shape, BF)
    barrier = pltpu.get_barrier_semaphore()

    def greet(to):
        pl.semaphore_signal(barrier, 1, device_id=to, device_id_type=MESH)

    around = [
        ((up, c), has_up),
        ((down, c), has_down),
        ((r, west), has_west),
        ((r, east), has_east),
        ((up, west), has_up & has_west),
        ((up, east), has_up & has_east),
        ((down, west), has_down & has_west),
        ((down, east), has_down & has_east),
    ]
    met = around[4:] + [((from_r, from_c), remote_main)]
    met += [(main_to(t, k), is_source & away(main_to(t, k))) for t in range(2) for k in range(2)]
    for d in range(1, COLS):
        greet((r, lax.rem(c + d, COLS)))
    peers = COLS - 1

    def gives(a, b):
        return ((a >= 2 * c - 1) & (a <= 2 * c + 2)) | (a == b + 1) | (a == b - 1)

    for d in range(1, ROWS):
        other = lax.rem(r + d, ROWS)
        there = gives(r, other) | gives(other, r)
        pl.when(there)(functools.partial(greet, (other, c)))
        peers = peers + jnp.where(there, 1, 0)
    for to, there in met:
        pl.when(there)(functools.partial(greet, to))
        peers = peers + jnp.where(there, 1, 0)

    def copy(source, target, out_sem, in_sem, to):
        return pltpu.make_async_remote_copy(
            src_ref=source,
            dst_ref=target,
            send_sem=out_sem,
            recv_sem=in_sem,
            device_id=to,
            device_id_type=MESH,
        )

    def piece(j, k):
        t, q = j // 4, lax.rem(j, 4)
        return copy(pieces.at[k, t, pl.ds(4 * q, 4)], got.at[pl.ds(4 * q, 4)],
                    send.at[2 * j + k], recv.at[q], main_to(t, k))

    def stay(j, k):
        t, q = j // 4, lax.rem(j, 4)
        return pltpu.make_async_copy(
            pieces.at[k, t, pl.ds(4 * q, 4)], got.at[pl.ds(4 * q, 4)], own.at[q]
        )

    for y in loads[1:3]:
        y.wait()
    place = r * COLS + c
    gathered[place] = jnp.concatenate([feats[0], feats[1]], axis=1)
    pl.semaphore_wait(barrier, peers)
    first = [
        copy(gathered.at[place], gathered.at[place], send_a.at[d], recv_a.at[d],
             (r, lax.rem(c + d, COLS)))
        for d in range(1, COLS)
    ]
    for y in first:
        y.start()
    loads[0].wait()
    for q in range(4):
        tile[16 * q : 16 * q + 16] = jnp.swapaxes(whole[:, 16 * q : 16 * q + 16, :], 0, 1)
    sixteenth = lanes_of((64, 128)) // 16

    def pack_edges(q, carry):
        low = tile[8 * q]
        high = pltpu.roll(low, 16, 1)
        for k in range(1, 8):
            v = tile[8 * q + k]
            low = jnp.where(sixteenth == k, pltpu.roll(v, 16 * k, 1), low)
            high = jnp.where(sixteenth == k, pltpu.roll(v, (16 * k + 16) % 128, 1), high)
        left[q] = low
        right[q] = high
        return carry

    lax.fori_loop(0, 8, pack_edges, 0)
    outlines = [
        (right, rim_left.at[pl.ds(2, 8)], (r, east), has_east, has_west),
        (left, rim_right.at[pl.ds(2, 8)], (r, west), has_west, has_east),
        (tile.at[pl.ds(54, 10)], rows.at[0], (down, c), has_down, has_up),
        (tile.at[pl.ds(0, 10)], rows.at[1], (up, c), has_up, has_down),
        (right.at[pl.ds(6, 2)], rim_left.at[pl.ds(0, 2)], (down, east),
         has_down & has_east, has_up & has_west),
        (right.at[pl.ds(0, 2)], rim_left.at[pl.ds(10, 2)], (up, east),
         has_up & has_east, has_down & has_west),
        (left.at[pl.ds(6, 2)], rim_right.at[pl.ds(0, 2)], (down, west),
         has_down & has_west, has_up & has_east),
        (left.at[pl.ds(0, 2)], rim_right.at[pl.ds(10, 2)], (up, west),
         has_up & has_west, has_down & has_east),
    ]
    outlines = [
        (copy(s, t, send_f.at[k], recv_f.at[k], to), out, into)
        for k, (s, t, to, out, into) in enumerate(outlines)
    ]
    for y, out, _ in outlines:
        pl.when(out)(y.start)
    for y in first:
        y.wait_recv()
    block = gathered.at[pl.ds(r * COLS, COLS)]
    second = [
        copy(block, block, send_b.at[d], recv_b.at[d], (lax.rem(r + d, ROWS), c))
        for d in range(1, ROWS)
    ]
    for d, y in enumerate(second, 1):
        pl.when(gives(r, lax.rem(r + d, ROWS)))(y.start)
    for y in loads[3:]:
        y.wait()
    joined = first_refine[...].reshape(192, 384)
    w3[...] = halves_joined(joined[:, 0:128], joined[:, 128:256], joined[:, 256:384], False)
    bias[0] = bias_columns(coarse_bias, 0, 256)
    bias[1] = bias_columns(coarse_bias, 1, 256)
    for d, y in enumerate(second, 1):
        pl.when(gives(lax.rem(r + ROWS - d, ROWS), r))(y.wait_recv)

    row0, col0 = r * TR, c * TC
    every_bin = gathered[...].reshape(SIDE, 128)
    picked = chosen_bins(every_bin, row0 - 24, False)
    fr[...] = picked[0:64]
    fine_r[...] = picked[64:128].astype(BF)
    picked = chosen_bins(every_bin, col0, True)
    fc[...] = picked[0:64]
    fine_c[...] = picked[64:128].astype(BF)
    w1 = weights[0].reshape(192, 192)
    w2 = weights[1].reshape(192, 192)
    cols = col0 + column_offsets((64, 256))
    in_cols = (cols >= 0) & (cols < SIDE)
    half_c, half_r = lax.rem(c, COLS // 2) * TC, lax.rem(r, ROWS // 2) * TR
    cols_q = half_c + column_offsets((64, 256))
    in_quarter = (cols_q >= 0) & (cols_q < SIDE // 2)
    low_half = lanes_of((64, 128)) < 64

    def pair_row(q, k, at, body, shift):
        rim = jnp.where(
            low_half,
            pltpu.roll(rim_right[q], (128 - 16 * k) % 128, 1),
            pltpu.roll(rim_left[q], 112 - 16 * k, 1),
        )
        prior = jnp.concatenate([body, rim], axis=1).astype(F32)
        value = prior + (fc[...] + shift[:, k : k + 1])
        grow = row0 + 8 * q + k - 16
        inside = in_cols & (grow >= 0) & (grow < SIDE)
        x[at] = jnp.where(inside, value, 0.0).astype(BF)

    def features_at(q):
        return pltpu.roll(fr[...], lax.rem(248 - 8 * q, 128), 1)

    def rim_rows(side):
        for k in range(10):
            row = 64 + k if side else k - 10
            q = (row + 16) // 8
            pair_row(q, row % 8, row + 10, rows[side, k], features_at(q))

    def own_rows(g):
        shift = features_at(g + 2)
        for k in range(8):
            pair_row(g + 2, k, 8 * g + k + 10, tile[8 * g + k], shift)

    def hidden_rows(first, taken, count):
        for t in range(count):
            at = first + t
            grow = row0 + at - 8
            value = jnp.maximum(tap_sum(taps1, taken + t, 2, 256) + bias[0], 0.0)
            inside = in_cols & (grow >= 0) & (grow < SIDE)
            hidden[at] = jnp.where(inside, value, 0.0).astype(BF)

    def field_rows(first, taken, count):
        for t in range(count):
            at = first + t
            qrow = half_r + at - 4
            value = jnp.maximum(tap_sum(taps2, taken + t, 4, 256) + bias[1], 0.0)
            inside = in_quarter & (qrow >= 0) & (qrow < SIDE // 2)
            fields[at] = jnp.where(inside, value, 0.0).astype(BF)

    def pack(j):
        t, q = j // 4, lax.rem(j, 4)
        for k in range(0, 8, 2):
            v = tap_sum(taps3, k, 4, 128).astype(BF)
            u = tap_sum(taps3, k + 1, 4, 128).astype(BF)
            at = 4 * q + k // 2
            pieces[0, t, at] = jnp.where(low_half, v, pltpu.roll(u, 64, 1))
            pieces[1, t, at] = jnp.where(low_half, pltpu.roll(v, 64, 1), u)

    for y, _, into in outlines:
        pl.when(into)(y.wait_recv)
    rim_rows(0)

    def early_rows(g, carry):
        own_rows(g)
        return carry

    lax.fori_loop(0, 2, early_rows, 0)
    tap_products(w1, x, 0, taps1, 0, 20, 10, 2, 256)
    hidden_rows(0, 0, 16)
    tap_products(w2, hidden, 0, taps2, 0, 16, 8, 4, 256)
    field_rows(0, 0, 8)
    tap_products(w3[...], fields, 0, taps3, 8, 8, 8, 4, 128)
    def chunk(j, carry):
        pl.when(j < 6)(lambda: own_rows(j + 2))
        pl.when(j == 6)(lambda: rim_rows(1))
        carry_taps(taps1, 2)
        carry_taps(taps2, 4)
        carry_taps(taps3, 4)
        tap_products(w1, x, 20 + 8 * j, taps1, 12, 8, 8, 2, 256)
        hidden_rows(16 + 8 * j, 8, 8)
        tap_products(w2, hidden, 16 + 8 * j, taps2, 8, 8, 8, 4, 256)
        field_rows(8 + 8 * j, 0, 8)
        tap_products(w3[...], fields, 8 + 8 * j, taps3, 8, 8, 8, 4, 128)
        pack(j)
        for k in range(2):
            pl.when(is_source & away(main_to(j // 4, k)))(lambda k=k: piece(j, k).start())
            pl.when(is_source & jnp.logical_not(away(main_to(j // 4, k))))(
                lambda k=k: stay(j, k).start()
            )
        return carry

    lax.fori_loop(0, 8, chunk, 0)
    for q in range(4):
        map_out[:, 16 * q : 16 * q + 16, :] = jnp.swapaxes(
            fields[4 + 16 * q : 20 + 16 * q, :, 0:128], 0, 1
        )

    store_map = pltpu.make_async_copy(map_out, map_result, load.at[0])
    store_map.start()

    wq = halves_joined(joined[:, 0:128], joined[:, 128:256], joined[:, 256:384], True)
    wp = jnp.concatenate(
        [
            halves_joined(*[first_refine[a, :, 128 * e : 128 * e + 128] for a in range(3)], True)
            for e in range(3)
        ],
        axis=0,
    )
    w4 = second_refine[...].reshape(192, 192)
    terms = jnp.dot(wq, shifted_stack(fine_c[...], 8, 256), preferred_element_type=F32)
    base = terms[64:128] + bias_columns(refine_bias, 0, 256)
    row_terms[0] = base + terms[0:64] + terms[128:192]
    row_terms[1] = base + terms[128:192]
    row_terms[2] = base + terms[0:64]
    stack = jnp.concatenate([pltpu.roll(fine_r[...], 8, 1), fine_r[...], pltpu.roll(fine_r[...], 120, 1)], axis=0)
    terms = jnp.dot(wp, stack, preferred_element_type=F32)
    row_part[0] = terms[0:64] + terms[64:128] + terms[128:192]
    row_part[1] = terms[64:128] + jnp.where(c == 0, terms[128:192], terms[0:64])
    bias[0] = bias_columns(refine_bias, 1, 256)

    def spread_main(source, first, count, at):
        for k in range(2):
            value = jnp.dot(
                source[first : first + count].reshape(count * 64, 128),
                main_table[k],
                preferred_element_type=F32,
            )
            wide[at : at + count, k, :, 0:128] = value.reshape(count, 64, 128).astype(BF)

    rims = [
        (got.at[pl.ds(0, 4)], bottom, (up, c), has_up, has_down, 0),
        (sides.at[0, 0], side_in.at[1, 1], (r, west), has_west, has_east, 1),
        (sides.at[1, 0], side_in.at[0, 1], (r, east), has_east, has_west, 1),
        (sides.at[0, 0], side_in.at[1, 3], (up, west),
         has_up & has_west, has_down & has_east, 1),
        (sides.at[1, 0], side_in.at[0, 3], (up, east),
         has_up & has_east, has_down & has_west, 1),
        (got.at[pl.ds(12, 4)], top, (down, c), has_down, has_up, 3),
        (sides.at[0, 1], side_in.at[1, 2], (r, west), has_west, has_east, 3),
        (sides.at[1, 1], side_in.at[0, 2], (r, east), has_east, has_west, 3),
        (sides.at[0, 1], side_in.at[1, 0], (down, west),
         has_down & has_west, has_up & has_east, 3),
        (sides.at[1, 1], side_in.at[0, 0], (down, east),
         has_down & has_east, has_up & has_west, 3),
    ]
    rims = [
        (copy(s, t, send_n.at[k], recv_n.at[k], to), out, into, when)
        for k, (s, t, to, out, into, when) in enumerate(rims)
    ]
    part = lanes_of((64, 128)) // 8

    def pack_sides(half_tile):
        low = high = None
        for k in range(16):
            v = got[8 * half_tile + k // 2]
            start = (8 * k - 64 * (k % 2)) % 128
            moved, other = pltpu.roll(v, start, 1), pltpu.roll(v, (start - 56) % 128, 1)
            low = moved if k == 0 else jnp.where(part == k, moved, low)
            high = other if k == 0 else jnp.where(part == k, other, high)
        sides[0, half_tile] = low
        sides[1, half_tile] = high

    offsets = column_offsets((64, 256)) + col0
    inside_of = [(offsets >= 0) & (offsets < SIDE)]
    edge_of = [(offsets < 8) | (offsets >= SIDE - 8)]

    def fine_rows(g, at):
        lanes = slice(at, at + 128)
        grow0 = row0 + 8 * g - 16
        inside = inside_of[0][:, lanes] & (grow0 >= 0) & (grow0 < SIDE)
        variant = jnp.where(grow0 == 0, 1, jnp.where(grow0 == SIDE - 8, 2, 0))
        shift = lax.rem(256 - 8 * g - 8, 128)
        everywhere = pltpu.roll(row_part[0], shift, 1)
        edge = pltpu.roll(row_part[1], shift, 1)
        column_terms = row_terms[variant, :, lanes]
        for k in range(8):
            row = jnp.where(edge_of[0][:, lanes], edge[:, k : k + 1], everywhere[:, k : k + 1])
            value = wide[2 * g + k // 4, (k // 2) % 2, :, lanes].astype(F32) + (column_terms + row)
            fine[8 * g + k, :, lanes] = jnp.where(inside, jnp.maximum(value, 0.0), 0.0).astype(BF)

    def own_fine_rows(g, carry):
        fine_rows(g, 0)
        return carry

    def side_fine_rows(g, carry):
        fine_rows(g, 128)
        return carry

    for q in range(4):
        pl.when(remote_main)(lambda: piece(q, 0).wait_recv())
        pl.when(jnp.logical_not(remote_main))(lambda: stay(q, 0).wait())
        if q % 2:
            pack_sides(q // 2)
        for y, out, _, when in rims:
            if when == q:
                pl.when(out)(y.start)
        spread_main(got, 4 * q, 4, 4 + 4 * q)
        lax.fori_loop(2 + 2 * q, 4 + 2 * q, own_fine_rows, 0)
    for y, _, into, _ in rims:
        pl.when(into)(y.wait_recv)
    spread_main(top, 0, 4, 0)
    spread_main(bottom, 0, 4, 20)

    def spread_rim(tile_at, low, high, first):
        both = jnp.concatenate(
            [
                jnp.where(has_east, side_in[1, tile_at].astype(F32), 0.0),
                jnp.where(has_west, side_in[0, tile_at].astype(F32), 0.0),
            ],
            axis=1,
        ).astype(BF)
        value = jnp.dot(
            both, rim_table[:, 128 * low : 128 * high], preferred_element_type=F32
        ).astype(BF)
        for k in range(high - low):
            row = first + k
            wide[row // 2, row % 2, :, 128:256] = value[:, 128 * k : 128 * k + 128]

    spread_rim(0, 8, 16, 0)
    spread_rim(1, 0, 16, 8)
    spread_rim(2, 0, 16, 24)
    spread_rim(3, 0, 8, 40)
    for g in (0, 1, 10, 11):
        fine_rows(g, 0)
    lax.fori_loop(0, 12, side_fine_rows, 0)

    def last_products(g, carry):
        tap_products(w4, fine, 16 * g, taps4, 16 * g, 16, 8, 16, 128)
        return carry

    lax.fori_loop(0, 6, last_products, 0)
    for g in range(4):
        value = jnp.stack(
            [
                jnp.maximum(tap_sum(taps4, 16 * g + k, 16, 128) + bias[0, :, 0:128], 0.0).astype(BF)
                for k in range(16)
            ]
        )
        refined[:, 16 * g : 16 * g + 16, :] = jnp.swapaxes(value, 0, 1)
    store_refined = pltpu.make_async_copy(refined, refined_result, load.at[1])
    store_refined.start()
    for y in first:
        y.wait_send()
    for d, y in enumerate(second, 1):
        pl.when(gives(r, lax.rem(r + d, ROWS)))(y.wait_send)
    for y, out, _ in outlines:
        pl.when(out)(y.wait_send)
    for j in range(8):
        for k in range(2):
            pl.when(is_source & away(main_to(j // 4, k)))(lambda: piece(j, k).wait_send())
    for y, out, _, _ in rims:
        pl.when(out)(y.wait_send)
    store_map.wait()
    store_refined.wait()


def decoder(half, *arguments):
    return pl.pallas_call(
        functools.partial(decoder_kernel, half),
        out_shape=(
            jax.ShapeDtypeStruct((64, TR, TC), BF),
            jax.ShapeDtypeStruct((64, TR, TC), BF),
        ),
        in_specs=[anywhere] * 10,
        out_specs=(anywhere, anywhere),
        scratch_shapes=[
            pltpu.VMEM((64, TR, TC), BF),
            pltpu.VMEM((2, 3, 64, 192), BF),
            pltpu.VMEM((3, 64, 384), BF),
            pltpu.VMEM((3, 64, 192), BF),
            pltpu.VMEM((2, 64), F32),
            pltpu.VMEM((2, 64), F32),
            pltpu.VMEM((2, 128, 128), BF),
            pltpu.VMEM((256, 2048), BF),
            pltpu.VMEM((TR, 64, TC), BF),
            pltpu.VMEM((2, 10, 64, TC), BF),
            pltpu.VMEM((12, 64, TC), BF),
            pltpu.VMEM((12, 64, TC), BF),
            pltpu.VMEM((8, 64, TC), BF),
            pltpu.VMEM((8, 64, TC), BF),
            pltpu.VMEM((2, 8, 64), BF),
            pltpu.VMEM((ROWS * COLS, 8, TC), BF),
            pltpu.VMEM((64, TR, TC), BF),
            pltpu.VMEM((64, TR, TC), BF),
            pltpu.VMEM((84, 64, 256), BF),
            pltpu.VMEM((20, 192, 256), F32),
            pltpu.VMEM((80, 64, 256), BF),
            pltpu.VMEM((16, 192, 256), F32),
            pltpu.VMEM((72, 64, 256), BF),
            pltpu.VMEM((16, 192, 128), F32),
            pltpu.VMEM((192, 192), BF),
            pltpu.VMEM((2, 64, 256), F32),
            pltpu.VMEM((64, 128), F32),
            pltpu.VMEM((64, 256), F32),
            pltpu.VMEM((64, 128), BF),
            pltpu.VMEM((64, 256), BF),
            pltpu.VMEM((2, 2, 16, 64, 128), BF),
            pltpu.VMEM((16, 64, 128), BF),
            pltpu.VMEM((2, 2, 64, 128), BF),
            pltpu.VMEM((4, 64, 128), BF),
            pltpu.VMEM((4, 64, 128), BF),
            pltpu.VMEM((2, 4, 64, 128), BF),
            pltpu.VMEM((24, 2, 64, 256), BF),
            pltpu.VMEM((96, 64, 256), BF),
            pltpu.VMEM((96, 192, 128), F32),
            pltpu.VMEM((3, 64, 256), F32),
            pltpu.VMEM((2, 64, 128), F32),
            pltpu.SemaphoreType.DMA((16,)),
            pltpu.SemaphoreType.DMA((4,)),
            pltpu.SemaphoreType.DMA((4,)),
            pltpu.SemaphoreType.DMA((10,)),
            pltpu.SemaphoreType.DMA((10,)),
            pltpu.SemaphoreType.DMA((10,)),
            pltpu.SemaphoreType.DMA((8,)),
            pltpu.SemaphoreType.DMA((8,)),
            pltpu.SemaphoreType.DMA((COLS,)),
            pltpu.SemaphoreType.DMA((COLS,)),
            pltpu.SemaphoreType.DMA((ROWS,)),
            pltpu.SemaphoreType.DMA((ROWS,)),
        ],
        compiler_params=pltpu.CompilerParams(
            collective_id=2 + half, has_side_effects=True, vmem_limit_bytes=VMEM_BYTES
        ),
    )(*arguments)


def per_device(coarse_feats, fine_feats, pair_prior, zoom_start, coarse_weights, coarse_bias,
               refine_first, refine_second, refine_bias):
    main_table, rim_table = spread_tables()
    return lax.cond(
        zoom_start[0] == 0,
        functools.partial(decoder, 0),
        functools.partial(decoder, 1),
        coarse_feats.T, fine_feats.T, pair_prior, coarse_weights, refine_first, refine_second,
        coarse_bias, refine_bias, jnp.asarray(main_table, BF), jnp.asarray(rim_table, BF),
    )


def solution(mesh):
    return jax.shard_map(
        per_device,
        mesh=mesh,
        in_specs=(
            P(None, ("row", "col")),
            P(None, ("row", "col")),
            P(None, "row", "col"),
            P(),
            P(),
            P(),
            P(),
            P(),
            P(),
        ),
        out_specs=(P(None, "row", "col"), P(None, "row", "col")),
        check_vma=False,
    )
```

```python
import functools

import jax
import jax.numpy as jnp
import numpy as np
from jax import lax
from jax.experimental import pallas as pl
from jax.experimental.pallas import tpu as pltpu
from jax.sharding import PartitionSpec as P

BF = jnp.bfloat16
F32 = jnp.float32
MESH = pl.DeviceIdType.MESH
VMEM_BYTES = 58 << 20
SIDE = 1024
ROWS, COLS = 16, 8
TR, TC = 64, 128

anywhere = pl.BlockSpec(memory_space=pl.ANY)


def lanes_of(shape):
    return lax.broadcasted_iota(jnp.int32, shape, len(shape) - 1)


def column_offsets(shape):
    lane = lanes_of(shape)
    return jnp.where(lane < 192, lane, lane - 256)


def shifted_stack(x, spacing, width):
    return jnp.concatenate(
        [
            pltpu.roll(x, spacing, 1)[:, :width],
            x[:, :width],
            pltpu.roll(x, 256 - spacing, 1)[:, :width],
        ],
        axis=0,
    )


def tap_products(w, source, first, target, into, count, group, spacing, width):
    for g in range(count // group):
        base = first + g * group
        stack = jnp.concatenate(
            [shifted_stack(source[base + t], spacing, width) for t in range(group)], axis=1
        )
        product = jnp.dot(w, stack, preferred_element_type=F32)
        for t in range(group):
            target[into + g * group + t] = product[:, t * width : (t + 1) * width]


def carry_taps(target, spacing):
    for t in range(2 * spacing):
        last = target.shape[0] - 2 * spacing + t
        target[last - 8, 0:64] = target[last, 0:64]
        if t >= spacing:
            target[last - 8, 64:128] = target[last, 64:128]


def tap_sum(target, i, spacing, width):
    return (
        target[i, 0:64, 0:width]
        + target[i + spacing, 64:128, 0:width]
        + target[i + 2 * spacing, 128:192, 0:width]
    )


def bias_columns(bias, layer, width):
    row = jnp.broadcast_to(bias[layer : layer + 1, :], (128, 64))
    column = jnp.transpose(row)
    return column if width == 128 else jnp.concatenate([column, column], axis=1)


def halves_joined(a, b, c, upper):
    low = lanes_of(a.shape) < 64
    if upper:
        first = jnp.where(low, pltpu.roll(a, 64, 1), b)
        return jnp.concatenate([first, pltpu.roll(c, 64, 1)[:, :64]], axis=1)
    first = jnp.where(low, a, pltpu.roll(b, 64, 1))
    return jnp.concatenate([first, c[:, :64]], axis=1)


def chosen_bins(gathered, first, ring):
    lanes = 256 if ring else 128
    shape = (SIDE, lanes)
    wanted = first + (column_offsets(shape) if ring else lanes_of(shape))
    picked = lax.broadcasted_iota(jnp.int32, shape, 0) == wanted
    return lax.dot_general(
        gathered,
        jnp.where(picked, 1.0, 0.0).astype(BF),
        (((0,), (0,)), ((), ())),
        preferred_element_type=F32,
    )


def spread_tables():
    lane = np.arange(128)
    source = np.arange(128)[:, None]
    main = np.stack([source == 64 * k + lane[None] // 2 for k in range(2)])
    rim = np.zeros((256, 16, 128), bool)
    for k in range(16):
        rim[:128, k] = (source == 8 * k + lane[None] // 2) & (lane[None] < 16)
        rim[128:, k] = (source == 8 * k + (lane[None] - 112) // 2) & (lane[None] >= 112)
    return main.astype(np.float32), rim.reshape(256, 2048).astype(np.float32)


def decoder_kernel(half, coarse_feats, fine_feats, prior, coarse_weights, first_weights,
                   second_weights, coarse_biases, refine_biases, tables_main, tables_rim,
                   map_result, refined_result,
                   whole, weights, first_refine, second_refine, coarse_bias, refine_bias,
                   main_table, rim_table,
                   tile, rows, rim_left, rim_right, left, right, feats, gathered, map_out, refined,
                   x, taps1, hidden, taps2, fields, taps3, w3, bias, fr, fc, fine_r, fine_c, pieces,
                   got, sides, top, bottom, side_in, wide, fine, taps4, row_terms, row_part,
                   send, recv, own, send_n, recv_n,
                   load, send_f, recv_f, send_a, recv_a, send_b, recv_b):
    loads = [
        (prior, whole),
        (coarse_feats, feats.at[0]),
        (fine_feats, feats.at[1]),
        (coarse_weights, weights),
        (first_weights, first_refine),
        (second_weights, second_refine),
        (coarse_biases, coarse_bias),
        (refine_biases, refine_bias),
        (tables_main, main_table),
        (tables_rim, rim_table),
    ]
    loads = [pltpu.make_async_copy(s, d, load.at[k]) for k, (s, d) in enumerate(loads)]
    for y in loads:
        y.start()
    r, c = lax.axis_index("row"), lax.axis_index("col")
    base_r, base_c = half * (ROWS // 2), half * (COLS // 2)
    up, down = lax.rem(r + ROWS - 1, ROWS), lax.rem(r + 1, ROWS)
    west, east = lax.rem(c + COLS - 1, COLS), lax.rem(c + 1, COLS)
    has_up, has_down, has_west, has_east = r > 0, r < ROWS - 1, c > 0, c < COLS - 1
    from_r, from_c = base_r + r // 2, base_c + c // 2
    remote_main = (from_r != r) | (from_c != c)
    is_source = (r >= base_r) & (r < base_r + ROWS // 2) & (c >= base_c) & (c < base_c + COLS // 2)
    local_r, local_c = r - base_r, c - base_c

    def main_to(t, h):
        return 2 * local_r + t, 2 * local_c + h

    def away(to):
        return (to[0] != r) | (to[1] != c)

    gathered[...] = jnp.zeros(gathered.shape, BF)
    barrier = pltpu.get_barrier_semaphore()

    def greet(to):
        pl.semaphore_signal(barrier, 1, device_id=to, device_id_type=MESH)

    around = [
        ((up, c), has_up),
        ((down, c), has_down),
        ((r, west), has_west),
        ((r, east), has_east),
        ((up, west), has_up & has_west),
        ((up, east), has_up & has_east),
        ((down, west), has_down & has_west),
        ((down, east), has_down & has_east),
    ]
    met = around[4:] + [((from_r, from_c), remote_main)]
    met += [(main_to(t, k), is_source & away(main_to(t, k))) for t in range(2) for k in range(2)]
    for d in range(1, COLS):
        greet((r, lax.rem(c + d, COLS)))
    peers = COLS - 1

    def gives(a, b):
        return ((a >= 2 * c - 1) & (a <= 2 * c + 2)) | (a == b + 1) | (a == b - 1)

    for d in range(1, ROWS):
        other = lax.rem(r + d, ROWS)
        there = gives(r, other) | gives(other, r)
        pl.when(there)(functools.partial(greet, (other, c)))
        peers = peers + jnp.where(there, 1, 0)
    for to, there in met:
        pl.when(there)(functools.partial(greet, to))
        peers = peers + jnp.where(there, 1, 0)

    def copy(source, target, out_sem, in_sem, to):
        return pltpu.make_async_remote_copy(
            src_ref=source,
            dst_ref=target,
            send_sem=out_sem,
            recv_sem=in_sem,
            device_id=to,
            device_id_type=MESH,
        )

    def piece(j, k):
        t, q = j // 4, lax.rem(j, 4)
        return copy(pieces.at[k, t, pl.ds(4 * q, 4)], got.at[pl.ds(4 * q, 4)],
                    send.at[2 * j + k], recv.at[q], main_to(t, k))

    def stay(j, k):
        t, q = j // 4, lax.rem(j, 4)
        return pltpu.make_async_copy(
            pieces.at[k, t, pl.ds(4 * q, 4)], got.at[pl.ds(4 * q, 4)], own.at[q]
        )

    for y in loads[1:3]:
        y.wait()
    place = r * COLS + c
    gathered[place] = jnp.concatenate([feats[0], feats[1]], axis=1)
    pl.semaphore_wait(barrier, peers)
    first = [
        copy(gathered.at[place], gathered.at[place], send_a.at[d], recv_a.at[d],
             (r, lax.rem(c + d, COLS)))
        for d in range(1, COLS)
    ]
    for y in first:
        y.start()
    loads[0].wait()
    for q in range(4):
        tile[16 * q : 16 * q + 16] = jnp.swapaxes(whole[:, 16 * q : 16 * q + 16, :], 0, 1)
    sixteenth = lanes_of((64, 128)) // 16

    def pack_edges(q, carry):
        low = tile[8 * q]
        high = pltpu.roll(low, 16, 1)
        for k in range(1, 8):
            v = tile[8 * q + k]
            low = jnp.where(sixteenth == k, pltpu.roll(v, 16 * k, 1), low)
            high = jnp.where(sixteenth == k, pltpu.roll(v, (16 * k + 16) % 128, 1), high)
        left[q] = low
        right[q] = high
        return carry

    lax.fori_loop(0, 8, pack_edges, 0)
    outlines = [
        (right, rim_left.at[pl.ds(2, 8)], (r, east), has_east, has_west),
        (left, rim_right.at[pl.ds(2, 8)], (r, west), has_west, has_east),
        (tile.at[pl.ds(54, 10)], rows.at[0], (down, c), has_down, has_up),
        (tile.at[pl.ds(0, 10)], rows.at[1], (up, c), has_up, has_down),
        (right.at[pl.ds(6, 2)], rim_left.at[pl.ds(0, 2)], (down, east),
         has_down & has_east, has_up & has_west),
        (right.at[pl.ds(0, 2)], rim_left.at[pl.ds(10, 2)], (up, east),
         has_up & has_east, has_down & has_west),
        (left.at[pl.ds(6, 2)], rim_right.at[pl.ds(0, 2)], (down, west),
         has_down & has_west, has_up & has_east),
        (left.at[pl.ds(0, 2)], rim_right.at[pl.ds(10, 2)], (up, west),
         has_up & has_west, has_down & has_east),
    ]
    outlines = [
        (copy(s, t, send_f.at[k], recv_f.at[k], to), out, into)
        for k, (s, t, to, out, into) in enumerate(outlines)
    ]
    for y, out, _ in outlines:
        pl.when(out)(y.start)
    for y in first:
        y.wait_recv()
    block = gathered.at[pl.ds(r * COLS, COLS)]
    second = [
        copy(block, block, send_b.at[d], recv_b.at[d], (lax.rem(r + d, ROWS), c))
        for d in range(1, ROWS)
    ]
    for d, y in enumerate(second, 1):
        pl.when(gives(r, lax.rem(r + d, ROWS)))(y.start)
    for y in loads[3:]:
        y.wait()
    joined = first_refine[...].reshape(192, 384)
    w3[...] = halves_joined(joined[:, 0:128], joined[:, 128:256], joined[:, 256:384], False)
    bias[0] = bias_columns(coarse_bias, 0, 256)
    bias[1] = bias_columns(coarse_bias, 1, 256)
    for d, y in enumerate(second, 1):
        pl.when(gives(lax.rem(r + ROWS - d, ROWS), r))(y.wait_recv)

    row0, col0 = r * TR, c * TC
    every_bin = gathered[...].reshape(SIDE, 128)
    picked = chosen_bins(every_bin, row0 - 24, False)
    fr[...] = picked[0:64]
    fine_r[...] = picked[64:128].astype(BF)
    picked = chosen_bins(every_bin, col0, True)
    fc[...] = picked[0:64]
    fine_c[...] = picked[64:128].astype(BF)
    w1 = weights[0].reshape(192, 192)
    w2 = weights[1].reshape(192, 192)
    cols = col0 + column_offsets((64, 256))
    in_cols = (cols >= 0) & (cols < SIDE)
    half_c, half_r = lax.rem(c, COLS // 2) * TC, lax.rem(r, ROWS // 2) * TR
    cols_q = half_c + column_offsets((64, 256))
    in_quarter = (cols_q >= 0) & (cols_q < SIDE // 2)
    low_half = lanes_of((64, 128)) < 64

    def pair_row(q, k, at, body, shift):
        rim = jnp.where(
            low_half,
            pltpu.roll(rim_right[q], (128 - 16 * k) % 128, 1),
            pltpu.roll(rim_left[q], 112 - 16 * k, 1),
        )
        prior = jnp.concatenate([body, rim], axis=1).astype(F32)
        value = prior + (fc[...] + shift[:, k : k + 1])
        grow = row0 + 8 * q + k - 16
        inside = in_cols & (grow >= 0) & (grow < SIDE)
        x[at] = jnp.where(inside, value, 0.0).astype(BF)

    def features_at(q):
        return pltpu.roll(fr[...], lax.rem(248 - 8 * q, 128), 1)

    def rim_rows(side):
        for k in range(10):
            row = 64 + k if side else k - 10
            q = (row + 16) // 8
            pair_row(q, row % 8, row + 10, rows[side, k], features_at(q))

    def own_rows(g):
        shift = features_at(g + 2)
        for k in range(8):
            pair_row(g + 2, k, 8 * g + k + 10, tile[8 * g + k], shift)

    def hidden_rows(first, taken, count):
        for t in range(count):
            at = first + t
            grow = row0 + at - 8
            value = jnp.maximum(tap_sum(taps1, taken + t, 2, 256) + bias[0], 0.0)
            inside = in_cols & (grow >= 0) & (grow < SIDE)
            hidden[at] = jnp.where(inside, value, 0.0).astype(BF)

    def field_rows(first, taken, count):
        for t in range(count):
            at = first + t
            qrow = half_r + at - 4
            value = jnp.maximum(tap_sum(taps2, taken + t, 4, 256) + bias[1], 0.0)
            inside = in_quarter & (qrow >= 0) & (qrow < SIDE // 2)
            fields[at] = jnp.where(inside, value, 0.0).astype(BF)

    def pack(j):
        t, q = j // 4, lax.rem(j, 4)
        for k in range(0, 8, 2):
            v = tap_sum(taps3, k, 4, 128).astype(BF)
            u = tap_sum(taps3, k + 1, 4, 128).astype(BF)
            at = 4 * q + k // 2
            pieces[0, t, at] = jnp.where(low_half, v, pltpu.roll(u, 64, 1))
            pieces[1, t, at] = jnp.where(low_half, pltpu.roll(v, 64, 1), u)

    for y, _, into in outlines:
        pl.when(into)(y.wait_recv)
    rim_rows(0)

    def early_rows(g, carry):
        own_rows(g)
        return carry

    lax.fori_loop(0, 2, early_rows, 0)
    tap_products(w1, x, 0, taps1, 0, 20, 10, 2, 256)
    hidden_rows(0, 0, 16)
    tap_products(w2, hidden, 0, taps2, 0, 16, 8, 4, 256)
    field_rows(0, 0, 8)
    tap_products(w3[...], fields, 0, taps3, 8, 8, 8, 4, 128)
    def chunk(j, carry):
        pl.when(j < 6)(lambda: own_rows(j + 2))
        pl.when(j == 6)(lambda: rim_rows(1))
        carry_taps(taps1, 2)
        carry_taps(taps2, 4)
        carry_taps(taps3, 4)
        tap_products(w1, x, 20 + 8 * j, taps1, 12, 8, 8, 2, 256)
        hidden_rows(16 + 8 * j, 8, 8)
        tap_products(w2, hidden, 16 + 8 * j, taps2, 8, 8, 8, 4, 256)
        field_rows(8 + 8 * j, 0, 8)
        tap_products(w3[...], fields, 8 + 8 * j, taps3, 8, 8, 8, 4, 128)
        pack(j)
        for k in range(2):
            pl.when(is_source & away(main_to(j // 4, k)))(lambda k=k: piece(j, k).start())
            pl.when(is_source & jnp.logical_not(away(main_to(j // 4, k))))(
                lambda k=k: stay(j, k).start()
            )
        return carry

    lax.fori_loop(0, 8, chunk, 0)
    for q in range(4):
        map_out[:, 16 * q : 16 * q + 16, :] = jnp.swapaxes(
            fields[4 + 16 * q : 20 + 16 * q, :, 0:128], 0, 1
        )

    store_map = pltpu.make_async_copy(map_out, map_result, load.at[0])
    store_map.start()

    wq = halves_joined(joined[:, 0:128], joined[:, 128:256], joined[:, 256:384], True)
    wp = jnp.concatenate(
        [
            halves_joined(*[first_refine[a, :, 128 * e : 128 * e + 128] for a in range(3)], True)
            for e in range(3)
        ],
        axis=0,
    )
    w4 = second_refine[...].reshape(192, 192)
    terms = jnp.dot(wq, shifted_stack(fine_c[...], 8, 256), preferred_element_type=F32)
    base = terms[64:128] + bias_columns(refine_bias, 0, 256)
    row_terms[0] = base + terms[0:64] + terms[128:192]
    row_terms[1] = base + terms[128:192]
    row_terms[2] = base + terms[0:64]
    stack = jnp.concatenate([pltpu.roll(fine_r[...], 8, 1), fine_r[...], pltpu.roll(fine_r[...], 120, 1)], axis=0)
    terms = jnp.dot(wp, stack, preferred_element_type=F32)
    row_part[0] = terms[0:64] + terms[64:128] + terms[128:192]
    row_part[1] = terms[64:128] + jnp.where(c == 0, terms[128:192], terms[0:64])
    bias[0] = bias_columns(refine_bias, 1, 256)

    def spread_main(source, first, count, at):
        for k in range(2):
            value = jnp.dot(
                source[first : first + count].reshape(count * 64, 128),
                main_table[k],
                preferred_element_type=F32,
            )
            wide[at : at + count, k, :, 0:128] = value.reshape(count, 64, 128).astype(BF)

    rims = [
        (got.at[pl.ds(0, 4)], bottom, (up, c), has_up, has_down, 0),
        (sides.at[0, 0], side_in.at[1, 1], (r, west), has_west, has_east, 1),
        (sides.at[1, 0], side_in.at[0, 1], (r, east), has_east, has_west, 1),
        (sides.at[0, 0], side_in.at[1, 3], (up, west),
         has_up & has_west, has_down & has_east, 1),
        (sides.at[1, 0], side_in.at[0, 3], (up, east),
         has_up & has_east, has_down & has_west, 1),
        (got.at[pl.ds(12, 4)], top, (down, c), has_down, has_up, 3),
        (sides.at[0, 1], side_in.at[1, 2], (r, west), has_west, has_east, 3),
        (sides.at[1, 1], side_in.at[0, 2], (r, east), has_east, has_west, 3),
        (sides.at[0, 1], side_in.at[1, 0], (down, west),
         has_down & has_west, has_up & has_east, 3),
        (sides.at[1, 1], side_in.at[0, 0], (down, east),
         has_down & has_east, has_up & has_west, 3),
    ]
    rims = [
        (copy(s, t, send_n.at[k], recv_n.at[k], to), out, into, when)
        for k, (s, t, to, out, into, when) in enumerate(rims)
    ]
    part = lanes_of((64, 128)) // 8

    def pack_sides(half_tile):
        low = high = None
        for k in range(16):
            v = got[8 * half_tile + k // 2]
            start = (8 * k - 64 * (k % 2)) % 128
            moved, other = pltpu.roll(v, start, 1), pltpu.roll(v, (start - 56) % 128, 1)
            low = moved if k == 0 else jnp.where(part == k, moved, low)
            high = other if k == 0 else jnp.where(part == k, other, high)
        sides[0, half_tile] = low
        sides[1, half_tile] = high

    offsets = column_offsets((64, 256)) + col0
    inside_of = [(offsets >= 0) & (offsets < SIDE)]
    edge_of = [(offsets < 8) | (offsets >= SIDE - 8)]

    def fine_rows(g, at):
        lanes = slice(at, at + 128)
        grow0 = row0 + 8 * g - 16
        inside = inside_of[0][:, lanes] & (grow0 >= 0) & (grow0 < SIDE)
        variant = jnp.where(grow0 == 0, 1, jnp.where(grow0 == SIDE - 8, 2, 0))
        shift = lax.rem(256 - 8 * g - 8, 128)
        everywhere = pltpu.roll(row_part[0], shift, 1)
        edge = pltpu.roll(row_part[1], shift, 1)
        column_terms = row_terms[variant, :, lanes]
        for k in range(8):
            row = jnp.where(edge_of[0][:, lanes], edge[:, k : k + 1], everywhere[:, k : k + 1])
            value = wide[2 * g + k // 4, (k // 2) % 2, :, lanes].astype(F32) + (column_terms + row)
            fine[8 * g + k, :, lanes] = jnp.where(inside, jnp.maximum(value, 0.0), 0.0).astype(BF)

    def own_fine_rows(g, carry):
        fine_rows(g, 0)
        return carry

    for q in range(4):
        pl.when(remote_main)(lambda: piece(q, 0).wait_recv())
        pl.when(jnp.logical_not(remote_main))(lambda: stay(q, 0).wait())
        if q % 2:
            pack_sides(q // 2)
        for y, out, _, when in rims:
            if when == q:
                pl.when(out)(y.start)
        spread_main(got, 4 * q, 4, 4 + 4 * q)
        lax.fori_loop(2 + 2 * q, 4 + 2 * q, own_fine_rows, 0)
    for y, _, into, _ in rims:
        pl.when(into)(y.wait_recv)
    spread_main(top, 0, 4, 0)
    spread_main(bottom, 0, 4, 20)

    def spread_rim(tile_at, low, high, first):
        both = jnp.concatenate(
            [
                jnp.where(has_east, side_in[1, tile_at].astype(F32), 0.0),
                jnp.where(has_west, side_in[0, tile_at].astype(F32), 0.0),
            ],
            axis=1,
        ).astype(BF)
        value = jnp.dot(
            both, rim_table[:, 128 * low : 128 * high], preferred_element_type=F32
        ).astype(BF)
        for k in range(high - low):
            row = first + k
            wide[row // 2, row % 2, :, 128:256] = value[:, 128 * k : 128 * k + 128]

    spread_rim(0, 8, 16, 0)
    spread_rim(1, 0, 16, 8)
    spread_rim(2, 0, 16, 24)
    spread_rim(3, 0, 8, 40)
    for g in (0, 1, 10, 11):
        fine_rows(g, 0)

    def last_products(g, carry):
        fine_rows(2 * g, 128)
        fine_rows(2 * g + 1, 128)
        tap_products(w4, fine, 16 * g, taps4, 16 * g, 16, 8, 16, 128)
        return carry

    lax.fori_loop(0, 6, last_products, 0)
    for g in range(4):
        value = jnp.stack(
            [
                jnp.maximum(tap_sum(taps4, 16 * g + k, 16, 128) + bias[0, :, 0:128], 0.0).astype(BF)
                for k in range(16)
            ]
        )
        refined[:, 16 * g : 16 * g + 16, :] = jnp.swapaxes(value, 0, 1)
    store_refined = pltpu.make_async_copy(refined, refined_result, load.at[1])
    store_refined.start()
    for y in first:
        y.wait_send()
    for d, y in enumerate(second, 1):
        pl.when(gives(r, lax.rem(r + d, ROWS)))(y.wait_send)
    for y, out, _ in outlines:
        pl.when(out)(y.wait_send)
    for j in range(8):
        for k in range(2):
            pl.when(is_source & away(main_to(j // 4, k)))(lambda: piece(j, k).wait_send())
    for y, out, _, _ in rims:
        pl.when(out)(y.wait_send)
    store_map.wait()
    store_refined.wait()


def decoder(half, *arguments):
    return pl.pallas_call(
        functools.partial(decoder_kernel, half),
        out_shape=(
            jax.ShapeDtypeStruct((64, TR, TC), BF),
            jax.ShapeDtypeStruct((64, TR, TC), BF),
        ),
        in_specs=[anywhere] * 10,
        out_specs=(anywhere, anywhere),
        scratch_shapes=[
            pltpu.VMEM((64, TR, TC), BF),
            pltpu.VMEM((2, 3, 64, 192), BF),
            pltpu.VMEM((3, 64, 384), BF),
            pltpu.VMEM((3, 64, 192), BF),
            pltpu.VMEM((2, 64), F32),
            pltpu.VMEM((2, 64), F32),
            pltpu.VMEM((2, 128, 128), BF),
            pltpu.VMEM((256, 2048), BF),
            pltpu.VMEM((TR, 64, TC), BF),
            pltpu.VMEM((2, 10, 64, TC), BF),
            pltpu.VMEM((12, 64, TC), BF),
            pltpu.VMEM((12, 64, TC), BF),
            pltpu.VMEM((8, 64, TC), BF),
            pltpu.VMEM((8, 64, TC), BF),
            pltpu.VMEM((2, 8, 64), BF),
            pltpu.VMEM((ROWS * COLS, 8, TC), BF),
            pltpu.VMEM((64, TR, TC), BF),
            pltpu.VMEM((64, TR, TC), BF),
            pltpu.VMEM((84, 64, 256), BF),
            pltpu.VMEM((20, 192, 256), F32),
            pltpu.VMEM((80, 64, 256), BF),
            pltpu.VMEM((16, 192, 256), F32),
            pltpu.VMEM((72, 64, 256), BF),
            pltpu.VMEM((16, 192, 128), F32),
            pltpu.VMEM((192, 192), BF),
            pltpu.VMEM((2, 64, 256), F32),
            pltpu.VMEM((64, 128), F32),
            pltpu.VMEM((64, 256), F32),
            pltpu.VMEM((64, 128), BF),
            pltpu.VMEM((64, 256), BF),
            pltpu.VMEM((2, 2, 16, 64, 128), BF),
            pltpu.VMEM((16, 64, 128), BF),
            pltpu.VMEM((2, 2, 64, 128), BF),
            pltpu.VMEM((4, 64, 128), BF),
            pltpu.VMEM((4, 64, 128), BF),
            pltpu.VMEM((2, 4, 64, 128), BF),
            pltpu.VMEM((24, 2, 64, 256), BF),
            pltpu.VMEM((96, 64, 256), BF),
            pltpu.VMEM((96, 192, 128), F32),
            pltpu.VMEM((3, 64, 256), F32),
            pltpu.VMEM((2, 64, 128), F32),
            pltpu.SemaphoreType.DMA((16,)),
            pltpu.SemaphoreType.DMA((4,)),
            pltpu.SemaphoreType.DMA((4,)),
            pltpu.SemaphoreType.DMA((10,)),
            pltpu.SemaphoreType.DMA((10,)),
            pltpu.SemaphoreType.DMA((10,)),
            pltpu.SemaphoreType.DMA((8,)),
            pltpu.SemaphoreType.DMA((8,)),
            pltpu.SemaphoreType.DMA((COLS,)),
            pltpu.SemaphoreType.DMA((COLS,)),
            pltpu.SemaphoreType.DMA((ROWS,)),
            pltpu.SemaphoreType.DMA((ROWS,)),
        ],
        compiler_params=pltpu.CompilerParams(
            collective_id=2 + half, has_side_effects=True, vmem_limit_bytes=VMEM_BYTES
        ),
    )(*arguments)


def per_device(coarse_feats, fine_feats, pair_prior, zoom_start, coarse_weights, coarse_bias,
               refine_first, refine_second, refine_bias):
    main_table, rim_table = spread_tables()
    return lax.cond(
        zoom_start[0] == 0,
        functools.partial(decoder, 0),
        functools.partial(decoder, 1),
        coarse_feats.T, fine_feats.T, pair_prior, coarse_weights, refine_first, refine_second,
        coarse_bias, refine_bias, jnp.asarray(main_table, BF), jnp.asarray(rim_table, BF),
    )


def solution(mesh):
    return jax.shard_map(
        per_device,
        mesh=mesh,
        in_specs=(
            P(None, ("row", "col")),
            P(None, ("row", "col")),
            P(None, "row", "col"),
            P(),
            P(),
            P(),
            P(),
            P(),
            P(),
        ),
        out_specs=(P(None, "row", "col"), P(None, "row", "col")),
        check_vma=False,
    )
```
